256 devices in a mesh: dp: 4 (over z_hi), expert: 64 (over y, x, z_lo, core).
Axes of the slice: x: 4, y: 4, z: 8 (z_hi: 4, z_lo: 2; z = z_hi * 2 + z_lo), core: 2. Of those that a mesh axis runs over, the one named last changes fastest.
Arguments:
- tokens: bfloat16 [32768, 3584], P(('dp', 'expert')), may hold values from -6 to 6
- cotangent: bfloat16 [32768, 1024], P(('dp', 'expert')), may hold values from -6 to 6
- expert_ids: int32 [32768, 8], P(('dp', 'expert')), may hold values from 0 to 255, all different within a row; in each aligned block of 128 rows (0 to 127, 128 to 255, ...) at most 6 rows name the same one
- gate_values: float32 [32768, 8], P(('dp', 'expert')), may hold values from 0.1 to 1
- counts: int32 [256], P(('dp', 'expert')), may hold values from 64 to 128
- swap_flags: int32 [64], replicated, may hold values from 0 to 1, as said below
- weights: bfloat16 [64, 3584, 1024], P('expert', 'dp'), may hold values from -0.035888672 to 0.035888672
- first_moment: bfloat16 [64, 3584, 1024], P('expert', 'dp'), may hold values from -6 to 6
- second_moment: bfloat16 [64, 3584, 1024], P('expert', 'dp'), may hold values from 1 to 100
Outputs:
- new_weights: bfloat16 [64, 3584, 1024], P('expert', 'dp')
- new_first: bfloat16 [64, 3584, 1024], P('expert', 'dp')
- new_second: bfloat16 [64, 3584, 1024], P('expert', 'dp')
The draws below stay inside these ranges and needn't reach their ends.
Inputs may be any that keep to these rules, and one draw needn't show every extreme that they name: `expert_ids`: within the 128 rows of one device no expert is named by more than 6 rows; a token names 8 different experts. swap_flags[e] equals swap_flags[(e + 32) mod 64].
All inputs are finite; a program needn't handle non-finite values.
Results may differ from the reference program's by a relative error of at most 0.015.
Values may be sent and summed in bfloat16 or wider, within the bound.
A program may use at most 128 MiB of HBM per device.

```python
import math
import jax
import jax.numpy as jnp
import numpy as np
from jax import lax

D = 3584
FF = 1024
TOPK = 8
TOK_DEV = 128
EXPERTS = 64
ALL_EXPERTS = 256
TOKENS = 32768
MOST = 6
N_DP = 4
N_EXPERT = 64


def draw_counts(key, part):
    total = N_DP * N_EXPERT
    values = jax.random.randint(jax.random.fold_in(key, 11), (total,), TOK_DEV // 2, TOK_DEV + 1)
    order = jax.random.permutation(jax.random.fold_in(key, 12), total)
    values = values.at[order[0]].set(TOK_DEV).at[order[1]].set(TOK_DEV // 2)
    return values.astype(jnp.int32)


def draw_swap_flags(key, part):
    pairs = EXPERTS // 2
    chosen = jax.random.randint(jax.random.fold_in(key, 21), (pairs,), 0, 2)
    order = jax.random.permutation(jax.random.fold_in(key, 22), pairs)
    chosen = chosen.at[order[0]].set(0).at[order[1]].set(1)
    return jnp.concatenate([chosen, chosen]).astype(jnp.int32)


def levels(own_key, dims, pieces, least, largest):
    loudness, own = 1.0, jax.random.fold_in(own_key, 6)
    for axis_at, blocks in pieces:
        heights = jnp.exp(jax.random.uniform(jax.random.fold_in(own, axis_at), (blocks,), jnp.float32, least / len(pieces), largest / len(pieces)))
        loudness = loudness * jnp.repeat(heights, dims[axis_at] // blocks).reshape([-1 if axis == axis_at else 1 for axis in range(len(dims))])
    return loudness


def routed_block(own_key, own, number, rows, count, top, most, lean):
    sequence = jax.random.permutation(own_key, count)
    packed, common = load_shares(count, rows * top, most, lean, True), load_shares(count, rows * top, most, lean, False)
    places = jnp.arange(count)

    def named(lengths, turn):
        used = int((lengths > 0).sum())
        fixed = max(1, used // 4)
        passed = fixed + (places - fixed + turn * (used - fixed)) % max(1, count - fixed)
        return jnp.zeros((count,), jnp.int32).at[sequence[jnp.where(places < fixed, places, passed)]].set(jnp.asarray(lengths, jnp.int32))

    lengths = jnp.where(number % 4 == 0, named(packed, number // 4), named(common, number - number // 4 - 1))
    mixed = jax.random.permutation(jax.random.fold_in(own, 3), count)
    donor, taker = mixed[0:count // 2 * 2:2], mixed[1:count // 2 * 2:2]
    margin = jnp.minimum(lengths[donor] - 1, most - lengths[taker]) // 2
    margin = jnp.where((donor == sequence[0]) | (taker == sequence[0]) | (lengths[taker] == 0), 0, jnp.maximum(margin, 0))
    passed = jax.random.randint(jax.random.fold_in(own, 4), (count // 2,), 0, 1 << 20) % (margin + 1)
    lengths = lengths.at[donor].add(-passed).at[taker].add(passed)
    members = jnp.searchsorted(jnp.cumsum(lengths), jnp.arange(rows * top), side="right").astype(jnp.int32)
    table = members.reshape(top, rows).T
    table = table[jax.random.permutation(jax.random.fold_in(own, 1), rows)]
    turn = jax.random.randint(jax.random.fold_in(own, 2), (rows, 1), 0, top)
    return jnp.take_along_axis(table, (jnp.arange(top)[None, :] + turn) % top, axis=1)


def load_shares(amount, total, limit, skew, full):
    loads = [(1 << 20) // math.isqrt(standing ** skew) + 1 for standing in range(1, amount + 1)]
    largest = limit if full else min(limit, max(-(-total // amount), total * loads[0] // sum(loads)))
    least = 1 if total - largest >= amount - 1 else 0
    holding, surplus = [largest] + [least] * (amount - 1), total - largest - least * (amount - 1)
    while surplus > 0:
        movable = [i for i in range(1, amount) if holding[i] < largest] or [i for i in range(1, amount) if holding[i] < limit]
        mass, left = sum([loads[i] for i in movable]), surplus
        for i in movable:
            more = min(limit - holding[i], max(1, left * loads[i] // mass), surplus)
            holding[i] = holding[i] + more
            surplus = surplus - more
    return np.array(holding)


def gaussian(key, dims, deviation, reach, split=(), held_as=jnp.bfloat16):
    entries = jax.random.normal(key, dims, jnp.float32) * deviation
    if len(split) > 0:
        entries = levels(key, dims, split, -0.22, 0.18) * entries
    return jnp.clip(entries, min=-reach, max=reach).astype(held_as)


def setup_inputs(seed: int = 0) -> dict:
    key_list = jax.random.split(jax.random.key(seed), 10)
    tokens = gaussian(key_list[0], (TOKENS, D), 1.0, 6.0, ((0, 256),))
    cotangent = gaussian(key_list[1], (TOKENS, FF), 1.0, 6.0, ((0, 256),))
    expert_ids_keys = jax.random.split(jax.random.fold_in(key_list[2], 1), TOKENS // TOK_DEV)
    expert_ids_turns = jax.random.permutation(jax.random.fold_in(key_list[2], 3), TOKENS // TOK_DEV)
    expert_ids = jax.vmap(lambda own, number: routed_block(jax.random.fold_in(key_list[2], 2), own, number, TOK_DEV, ALL_EXPERTS, TOPK, MOST, 2))(expert_ids_keys, expert_ids_turns).reshape((TOKENS, TOPK))
    gate_values = jnp.clip(jnp.exp(math.log(1.0) - 2.3025851 * jax.random.uniform(key_list[3], (TOKENS, TOPK), jnp.float32) ** levels(key_list[3], (TOKENS, TOPK), ((0, 256),), -0.2, 0.2)), 0.1, 1.0)
    counts = draw_counts(jax.random.fold_in(key_list[9], 71), 0)
    swap_flags = draw_swap_flags(jax.random.fold_in(key_list[9], 71), 0)
    weights = gaussian(key_list[6], (EXPERTS, D, FF), 0.006, 0.035888672, ((0, 64), (1, 4)))
    first_moment = gaussian(key_list[7], (EXPERTS, D, FF), 1.0, 6.0, ((0, 64), (1, 4)))
    second_moment = jnp.clip(jnp.exp(math.log(100.0) - 4.6051702 * jax.random.uniform(key_list[8], (EXPERTS, D, FF), jnp.float32) ** levels(key_list[8], (EXPERTS, D, FF), ((0, 64), (1, 4)), -0.2, 0.2)), 1.0, 100.0).astype(jnp.bfloat16)
    return {"tokens": tokens, "cotangent": cotangent, "expert_ids": expert_ids, "gate_values": gate_values, "counts": counts, "swap_flags": swap_flags, "weights": weights, "first_moment": first_moment, "second_moment": second_moment}


beta_first = 0.9
beta_second = 0.95
bias_first = 1.0 - 0.9 ** 3
bias_second = 1.0 - 0.95 ** 3
learn_rate = 0.005
epsilon = 1e-08

def slope_of(preact, gate_rows, cot_rows):
    sigm = jax.nn.sigmoid(preact)
    return (gate_rows[:, None] * cot_rows.astype(jnp.float32) * sigm * (1.0 + preact * (1.0 - sigm))).astype(jnp.bfloat16)

def adam_step(weight, first, second, grad):
    first_new = beta_first * first.astype(jnp.float32) + (1.0 - beta_first) * grad
    second_new = beta_second * second.astype(jnp.float32) + (1.0 - beta_second) * grad * grad
    ratio = first_new / bias_first / (jnp.sqrt(second_new / bias_second) + epsilon)
    wfull = weight.astype(jnp.float32)
    updated = (wfull - learn_rate * ratio).astype(jnp.bfloat16)
    return (updated, first_new.astype(jnp.bfloat16), second_new.astype(jnp.bfloat16))

def reference(tokens, cotangent, expert_ids, gate_values, counts, swap_flags, weights, first_moment, second_moment):
    groups = N_DP * N_EXPERT
    feats = tokens.reshape(groups, TOK_DEV, D).astype(jnp.float32)
    cots = cotangent.reshape(groups, TOK_DEV, FF).astype(jnp.float32)
    routed = expert_ids.reshape(groups, TOK_DEV, TOPK)
    gates = gate_values.reshape(groups, TOK_DEV, TOPK)
    live = jnp.arange(TOK_DEV, dtype=jnp.int32)[None, :] < counts[:, None]
    slot_range = jnp.arange(MOST, dtype=jnp.int32)

    def one_expert(expert):
        landed = ((routed == expert) & live[:, :, None]).astype(jnp.int32).reshape(groups, TOK_DEV * TOPK)
        ranked = jnp.cumsum(landed, axis=1) - landed
        slot_hits = ((ranked[:, :, None] == slot_range) & (landed[:, :, None] == 1)).astype(jnp.float32)
        slot_hits = slot_hits.reshape(groups, TOK_DEV, TOPK, MOST)
        picker = lax.optimization_barrier(jnp.sum(slot_hits, axis=2))
        gate_rows = jnp.einsum('gtks,gtk->gs', slot_hits, gates, precision=lax.Precision.HIGHEST).reshape(-1)
        row_feat = jnp.einsum('gts,gtd->gsd', picker, feats, precision=lax.Precision.HIGHEST).astype(jnp.bfloat16).reshape(-1, D)
        row_cot = jnp.einsum('gts,gtf->gsf', picker, cots, precision=lax.Precision.HIGHEST).astype(jnp.bfloat16).reshape(-1, FF)
        preact = jnp.dot(row_feat, weights[expert], preferred_element_type=jnp.float32)
        slope = slope_of(preact, gate_rows, row_cot)
        grad = jnp.dot(row_feat.T, slope, preferred_element_type=jnp.float32)
        return adam_step(weights[expert], first_moment[expert], second_moment[expert], grad)
    updated, first_new, second_new = lax.map(one_expert, jnp.arange(EXPERTS, dtype=jnp.int32))
    lanes = jnp.arange(EXPERTS, dtype=jnp.int32)
    partner = jnp.where(swap_flags == 1, (lanes + EXPERTS // 2) % EXPERTS, lanes)
    return (updated[partner], first_new[partner], second_new[partner])
```

```python
import jax
import jax.numpy as jnp
from jax import lax
from jax.sharding import PartitionSpec as P

beta_first = 0.9
beta_second = 0.95
bias_first = 1.0 - 0.9**3
bias_second = 1.0 - 0.95**3
learn_rate = 0.005
epsilon = 1e-08
most = 6
aux_cols = 128


def partner(block, axis, distance):
    count = lax.axis_size(axis)
    route = [(low, low ^ (1 << distance)) for low in range(count)]
    return lax.ppermute(block, axis, route)


def adam_step(weight, first, second, grad):
    first_new = beta_first * first.astype(jnp.float32) + (1.0 - beta_first) * grad
    second_new = beta_second * second.astype(jnp.float32) + (1.0 - beta_second) * grad * grad
    ratio = first_new / bias_first / (jnp.sqrt(second_new / bias_second) + epsilon)
    wfull = weight.astype(jnp.float32)
    updated = (wfull - learn_rate * ratio).astype(jnp.bfloat16)
    return (updated, first_new.astype(jnp.bfloat16), second_new.astype(jnp.bfloat16))


def routing(expert_ids, gate_values, counts, swap_flags, experts):
    tok_rows, top = expert_ids.shape
    lanes = jnp.arange(experts, dtype=jnp.int32)
    live = jnp.arange(tok_rows, dtype=jnp.int32)[:, None] < counts[0]
    named = [(expert_ids[:, k : k + 1] == lanes) & live for k in range(top)]
    every = sum(n.astype(jnp.float32) for n in named)
    earlier = jnp.tril(jnp.ones((tok_rows, tok_rows), jnp.bfloat16), -1)
    ranked = jnp.dot(earlier, every.astype(jnp.bfloat16), preferred_element_type=jnp.float32)
    half = experts // 2
    slot_of = jnp.where(swap_flags == 1, (lanes + half) % experts, lanes).astype(jnp.float32)
    target = jnp.stack([jnp.sum(jnp.where(n, slot_of + 1.0, 0.0), axis=1) for n in named], axis=1) - 1.0
    place = jnp.stack([jnp.sum(jnp.where(n, ranked, 0.0), axis=1) for n in named], axis=1)
    aux = jnp.concatenate([target, place, gate_values], axis=1)
    aux = jnp.pad(aux, ((0, 0), (0, aux_cols - 3 * top)))
    return aux.astype(jnp.bfloat16)


def shards(tokens, cotangent, expert_ids, gate_values, counts, swap_flags, weights, first_moment, second_moment):
    experts = lax.axis_size("expert")
    groups = lax.axis_size("dp")
    partner_bit = experts.bit_length() - 2
    tok_rows, width = tokens.shape
    hidden = cotangent.shape[1]
    top = expert_ids.shape[1]
    dpart, fpart = width // groups, hidden // groups
    lanes = jnp.arange(experts, dtype=jnp.int32)
    own_flag = jnp.sum(jnp.where(lanes == lax.axis_index("expert"), swap_flags, 0))

    moved_w = partner(weights, "expert", partner_bit)
    aux = routing(expert_ids, gate_values, counts, swap_flags, experts)
    blocks = jnp.stack(
        [
            jnp.concatenate(
                [tokens[:, r * dpart : (r + 1) * dpart], cotangent[:, r * fpart : (r + 1) * fpart], aux], axis=1
            )
            for r in range(groups)
        ]
    )
    recv = lax.all_to_all(blocks, "dp", split_axis=0, concat_axis=0, tiled=True)
    recv_rows = groups * tok_rows
    recv = recv.reshape(recv_rows, dpart + fpart + aux_cols)
    info = recv[:, dpart + fpart : dpart + fpart + 3 * top].astype(jnp.float32).T
    per_slot = groups * most
    group_base = (jnp.arange(recv_rows) // tok_rows * most).astype(jnp.float32)
    code = jnp.where(info[:top] >= 0, info[:top] * per_slot + info[top : 2 * top] + group_base, -1.0)
    gates = info[2 * top :]
    slots = lax.broadcasted_iota(jnp.int32, (experts * per_slot, recv_rows), 0).astype(jnp.float32)
    picker = jnp.zeros(slots.shape, jnp.float32)
    gated = jnp.zeros(slots.shape, jnp.float32)
    for k in range(top):
        hit = slots == code[k][None, :]
        picker = jnp.where(hit, 1.0, picker)
        gated = jnp.where(hit, gates[k][None, :], gated)
    xs = jnp.dot(picker.astype(jnp.bfloat16), recv[:, :dpart], preferred_element_type=jnp.float32)
    cs = jnp.dot(gated.astype(jnp.bfloat16), recv[:, dpart : dpart + fpart], preferred_element_type=jnp.float32)
    send = jnp.concatenate([xs.astype(jnp.bfloat16), cs.astype(jnp.bfloat16)], axis=1)
    send = send.reshape(experts, per_slot, dpart + fpart)
    got = lax.all_to_all(send, "expert", split_axis=0, concat_axis=0, tiled=True)
    got = got.reshape(experts * per_slot, dpart + fpart)
    x = got[:, :dpart]
    c = got[:, dpart:]

    moved_m = partner(first_moment, "expert", partner_bit)
    moved_v = partner(second_moment, "expert", partner_bit)
    weight = jnp.where(own_flag == 1, moved_w, weights)[0]
    zpart = jnp.stack(
        [
            jnp.dot(x, weight[:, r * fpart : (r + 1) * fpart], preferred_element_type=jnp.float32).astype(jnp.bfloat16)
            for r in range(groups)
        ]
    )
    z = lax.psum_scatter(zpart, "dp", scatter_dimension=0, tiled=False).astype(jnp.float32)
    sigm = jax.nn.sigmoid(z)
    slope = (c.astype(jnp.float32) * sigm * (1.0 + z * (1.0 - sigm))).astype(jnp.bfloat16)
    slopes = lax.all_gather(slope, "dp", axis=0, tiled=False)
    grad = jnp.concatenate(
        [
            lax.dot_general(x, slopes[r], (((0,), (0,)), ((), ())), preferred_element_type=jnp.float32)
            for r in range(groups)
        ],
        axis=1,
    )
    first = jnp.where(own_flag == 1, moved_m, first_moment)[0]
    second = jnp.where(own_flag == 1, moved_v, second_moment)[0]
    updated, first_new, second_new = adam_step(weight, first, second, grad)
    return (updated[None], first_new[None], second_new[None])


def solution(mesh):
    placed = (
        P(("dp", "expert"), None),
        P(("dp", "expert"), None),
        P(("dp", "expert"), None),
        P(("dp", "expert"), None),
        P(("dp", "expert")),
        P(),
        P("expert", "dp", None),
        P("expert", "dp", None),
        P("expert", "dp", None),
    )
    return jax.shard_map(
        shards,
        mesh=mesh,
        in_specs=placed,
        out_specs=(P("expert", "dp", None), P("expert", "dp", None), P("expert", "dp", None)),
        check_vma=False,
    )
```

```python
import functools

import jax
import jax.numpy as jnp
from jax import lax
from jax.experimental import pallas as pl
from jax.experimental.pallas import tpu as pltpu
from jax.sharding import PartitionSpec as P

beta_first = 0.9
beta_second = 0.95
bias_first = 1.0 - 0.9**3
bias_second = 1.0 - 0.95**3
learn_rate = 0.005
epsilon = 1e-08
most = 6
f32, bf16, i32 = jnp.float32, jnp.bfloat16, jnp.int32
MESH = pl.DeviceIdType.MESH
near_first = (0, 1, 3, 2)
pieces = 1
PART, PASS, FINISH, FORWARD, MOMENTS = range(5)
order = (
    (PART, 0), (PASS, 0), (PART, 1), (PASS, 1), (PART, 2), (MOMENTS, 0), (MOMENTS, 1), (FINISH, 0), (PASS, 2), (FINISH, 1), (FORWARD, 0), (PART, 3), (FORWARD, 1), (FINISH, 2), (PASS, 3), (FORWARD, 2), (FINISH, 3), (FORWARD, 3),
)


def exchange_kernel(
    nd, ne, planes,
    count, ids, gates, flags, tokens, cot, w, m, v,
    x_out, slopes, w_in, m_in, v_in,
    rx, aux, aux_in, places, weights, send, got, w_own, w_mov, z_send, z_own, z_first, z_right_in, z_left_in, own_slope,
    loc_sem, swap_send, swap_recv, ex_send, ex_recv, a_send, a_recv, f_send, f_recv, d_send, d_recv, r_send, r_recv,
):
    me_d, me_e = lax.axis_index("dp"), lax.axis_index("expert")
    right, left, opp = lax.rem(me_d + 1, nd), lax.rem(me_d + nd - 1, nd), lax.rem(me_d + 2, nd)
    mate = lax.rem(me_e + ne // 2, ne)
    top, tok_rows = ids.shape
    dpart, fpart = tokens.shape[1] // nd, cot.shape[1] // nd
    my_z = lax.rem(me_e // 2, 2)
    pair = me_e + 2 - 4 * my_z
    here = (me_e // 4) * 2 + lax.rem(me_e, 2)
    nh = ne // 2
    sources = 2 * nd
    per_slot = sources * most
    slots_plane = nh // planes
    my_plane = here // slots_plane

    def expert_at(spot):
        return (spot // 2) * 4 + 2 * my_z + lax.rem(spot, 2)

    rows_plane = slots_plane * per_slot
    half = rows_plane // 2

    barrier = pltpu.get_barrier_semaphore()

    def greet(i, carry):
        spot = lax.rem(here + i, nh)
        pl.semaphore_signal(barrier, inc=1, device_id={"expert": expert_at(spot)}, device_id_type=MESH)
        return carry

    lax.fori_loop(1, nh, greet, 0)
    others = [(i, e) for i in range(nd) for e in (me_e, pair)][1:]
    for i, e in others:
        pl.semaphore_signal(barrier, inc=1, device_id={"dp": lax.rem(me_d + i, nd), "expert": e}, device_id_type=MESH)
    pl.semaphore_wait(barrier, nh - 1 + len(others))

    def swap(kind, src, dst):
        return pltpu.make_async_remote_copy(
            src_ref=src, dst_ref=dst, send_sem=swap_send.at[kind], recv_sem=swap_recv.at[kind],
            device_id={"expert": mate}, device_id_type=MESH,
        )

    w_swap = swap(0, w.at[0], w_mov)

    def remote(src, dst, send_sem, recv_sem, dp, expert):
        return pltpu.make_async_remote_copy(
            src_ref=src, dst_ref=dst, send_sem=send_sem, recv_sem=recv_sem,
            device_id={"dp": dp, "expert": expert}, device_id_type=MESH,
        )

    def rows_from(dp, z):
        return pl.ds(pl.multiple_of((z * nd + dp) * tok_rows, tok_rows), tok_rows)

    my_rows = rows_from(me_d, my_z)
    side = lax.rem(me_d + nd - 1 + 2 * my_z, nd)

    def tok_cols(r):
        return pl.ds(pl.multiple_of(r * dpart, 128), dpart)

    def cot_cols(r):
        return pl.ds(pl.multiple_of(r * fpart, 128), fpart)

    exchanged = []
    low, high = me_e - 2 * my_z, me_e - 2 * my_z + 2
    split = tok_rows // 2
    parts = ((0, split, 0, dpart), (split, split, 0, dpart), (0, tok_rows, dpart, fpart))

    def part_of(kind, first):
        row, height, col, wide = parts[kind]
        return rx.at[pl.ds(pl.multiple_of(first + row, split), height), pl.ds(col, wide)]

    def first_row(dp, z):
        return (z * nd + dp) * tok_rows

    for kind, (row, height, col, wide) in enumerate(parts):
        for way, (dp, expert, number) in enumerate(
            ((opp, pair, 2), (right, low, my_z), (left, high, my_z), (me_d, pair, 3))
        ):
            src = tokens.at[pl.ds(row, height), tok_cols(dp)] if col == 0 else cot.at[:, cot_cols(dp)]
            dst = part_of(kind, first_row(me_d, my_z))
            copy = remote(src, dst, ex_send.at[kind, way], ex_recv.at[kind, number], dp, expert)
            copy.start()
            exchanged.append(copy)
    w_swap.start()
    own_x = pltpu.make_async_copy(tokens.at[:, tok_cols(me_d)], rx.at[my_rows, pl.ds(0, dpart)], loc_sem.at[0])
    own_c = pltpu.make_async_copy(cot.at[:, cot_cols(me_d)], rx.at[my_rows, pl.ds(dpart, fpart)], loc_sem.at[1])
    own_w = pltpu.make_async_copy(w.at[0], w_own, loc_sem.at[2])
    own_x.start()
    own_c.start()
    own_w.start()

    experts_col = lax.broadcasted_iota(i32, (ne, tok_rows), 0)
    live = lax.broadcasted_iota(i32, (ne, tok_rows), 1) < count[0]
    every = jnp.zeros((ne, tok_rows), f32)
    for k in range(top):
        every = every + jnp.where((ids[pl.ds(k, 1), :] == experts_col) & live, 1.0, 0.0)
    earlier = jnp.where(
        lax.broadcasted_iota(i32, (tok_rows, tok_rows), 0) < lax.broadcasted_iota(i32, (tok_rows, tok_rows), 1), 1.0, 0.0
    )
    ranked = jnp.dot(every.astype(bf16), earlier.astype(bf16), preferred_element_type=f32)
    flag_row = jnp.broadcast_to(flags[...], (ne, ne))
    expert_row = lax.broadcasted_iota(i32, (ne, ne), 0)
    flag_col = jnp.sum(jnp.where(expert_row == lax.broadcasted_iota(i32, (ne, ne), 1), flag_row, 0), axis=1, keepdims=True)
    expert_col = lax.broadcasted_iota(i32, (ne, 1), 0)
    slot_col = jnp.where(flag_col == 1, lax.rem(expert_col + ne // 2, ne), expert_col).astype(f32) + 1.0
    for k in range(top):
        hit = (ids[pl.ds(k, 1), :] == experts_col) & live
        slot = jnp.sum(jnp.where(hit, slot_col, 0.0), axis=0, keepdims=True)
        rank = jnp.sum(jnp.where(hit, ranked, 0.0), axis=0, keepdims=True)
        aux[pl.ds(k, 1), :] = slot - 1.0
        aux[pl.ds(top + k, 1), :] = rank + ((my_z * nd + me_d) * most + 1)
    aux[pl.ds(2 * top, top), :] = gates[...]
    my_source = my_z * nd + me_d
    aux_in[my_source] = aux[...]
    for n, (i, e) in enumerate(others):
        copy = remote(aux, aux_in.at[my_source], a_send.at[n], a_recv.at[n], lax.rem(me_d + i, nd), e)
        copy.start()
        exchanged.append(copy)

    for kind in range(len(parts)):
        for number, dp, z in ((1 - my_z, side, 1 - my_z), (my_z, side, my_z), (2, opp, 1 - my_z)):
            at = part_of(kind, first_row(dp, z))
            pltpu.make_async_copy(at, at, ex_recv.at[kind, number]).wait()
            copy = remote(at, at, f_send.at[kind, number], f_recv.at[kind, number], me_d, pair)
            copy.start()
            exchanged.append(copy)
    own_x.wait()
    own_c.wait()
    for kind in range(len(parts)):
        at = part_of(kind, 0)
        pltpu.make_async_copy(at, at, ex_recv.at[kind, 3]).wait()
        for number in range(3):
            pltpu.make_async_copy(at, at, f_recv.at[kind, number]).wait()
    for n in range(len(others)):
        pltpu.make_async_copy(aux, aux, a_recv.at[n]).wait()

    lanes = sources * tok_rows
    to_slot, to_row, gate = (
        jnp.concatenate([aux_in[g, pl.ds(part * top, top), :] for g in range(sources)], axis=1) for part in range(3)
    )
    slots = expert_at(lax.broadcasted_iota(i32, (nh, lanes), 0)).astype(f32)
    place = jnp.zeros((nh, lanes), f32)
    scale = jnp.zeros((nh, lanes), f32)
    for k in range(top):
        hit = slots == to_slot[k : k + 1]
        place = jnp.where(hit, to_row[k : k + 1], place)
        scale = jnp.where(hit, gate[k : k + 1], scale)
    places[...] = place
    weights[...] = scale
    my_at = pl.ds(pl.multiple_of(here * per_slot, per_slot), per_slot)

    def rows_of(slot):
        return pl.ds(pl.multiple_of(slot * per_slot, per_slot), per_slot)

    picked = (slots_plane, per_slot, lanes)
    number = (lax.broadcasted_iota(i32, picked, 1) + 1).astype(f32)
    for d in near_first:
        plane = lax.rem(my_plane + d, planes)
        plane_slots = pl.ds(pl.multiple_of(plane * slots_plane, slots_plane), slots_plane)
        hit = jnp.broadcast_to(places[plane_slots, :][:, None, :], picked) == number
        picker = jnp.where(hit, 1.0, 0.0).astype(bf16).reshape(rows_plane, lanes)
        gated = jnp.where(hit, jnp.broadcast_to(weights[plane_slots, :][:, None, :], picked), 0.0)
        gated = gated.astype(bf16).reshape(rows_plane, lanes)
        plane_rows = pl.ds(pl.multiple_of(plane * rows_plane, rows_plane), rows_plane)
        xs = jnp.dot(picker, rx[:, pl.ds(0, dpart)], preferred_element_type=f32)
        cs = jnp.dot(gated, rx[:, pl.ds(dpart, fpart)], preferred_element_type=f32)
        send[plane_rows, pl.ds(0, dpart)] = xs.astype(bf16)
        send[plane_rows, pl.ds(dpart, fpart)] = cs.astype(bf16)

        def dispatch(step, carry, d=d, plane=plane):
            slot = plane * slots_plane + lax.rem(here + step, slots_plane)
            pltpu.make_async_remote_copy(
                src_ref=send.at[rows_of(slot)], dst_ref=got.at[my_at],
                send_sem=d_send.at[d], recv_sem=d_recv.at[d],
                device_id={"expert": expert_at(slot)}, device_id_type=MESH,
            ).start()
            return carry

        lax.fori_loop(1 if d == 0 else 0, slots_plane, dispatch, 0)
    own_rows = pltpu.make_async_copy(send.at[my_at], got.at[my_at], loc_sem.at[3])
    own_rows.start()

    own_w.wait()
    w_swap.wait()
    steps = 7
    w_rows = w_own.shape[0] // steps

    mine = lax.broadcasted_iota(i32, (1, ne), 1) == me_e
    own_flag = jnp.sum(jnp.where(mine, flags[...], 0), axis=1, keepdims=True)

    def choose(i, carry):
        at = pl.ds(pl.multiple_of(i * w_rows, w_rows), w_rows)
        w_own[at] = jnp.where(own_flag == 1, w_mov[at].astype(f32), w_own[at].astype(f32)).astype(bf16)
        return carry

    lax.fori_loop(0, steps, choose, 0)
    w_save = pltpu.make_async_copy(w_own, w_in, loc_sem.at[4])
    w_save.start()

    def ring(kind, q, src, dst, to):
        return pltpu.make_async_remote_copy(
            src_ref=src, dst_ref=dst, send_sem=r_send.at[kind, q], recv_sem=r_recv.at[kind, q],
            device_id={"dp": to}, device_id_type=MESH,
        )

    head, tail = pl.ds(0, half), pl.ds(half, half)
    at_plane = [
        pl.multiple_of(lax.rem(my_plane + planes - d, planes) * rows_plane, rows_plane) for d in near_first
    ]
    pending = []

    def go(copy):
        copy.start()
        pending.append(copy)
        return copy

    copies = {}

    def bytes_of(blocks):
        return got.at[pl.ds(0, blocks * per_slot)]

    def partials(q):
        d = near_first[q]
        blocks = slots_plane - 1 if d == 0 else slots_plane
        pltpu.make_async_copy(bytes_of(blocks), bytes_of(blocks), d_recv.at[d]).wait()
        if d == 0:
            own_rows.wait()
        x = got[pl.ds(at_plane[q], rows_plane), pl.ds(0, dpart)]

        def part(r):
            cols = pl.ds(pl.multiple_of(r * fpart, 128), fpart)
            return jnp.dot(x, w_own[:, cols], preferred_element_type=f32)

        z_send[0, q] = part(opp).astype(bf16)
        copies[0, q] = go(ring(0, q, z_send.at[0, q, head], z_first.at[0, q], right))
        copies[1, q] = go(ring(1, q, z_send.at[0, q, tail], z_first.at[1, q], left))
        z_send[1, q] = part(right).astype(bf16)
        copies[2, q] = go(ring(2, q, z_send.at[1, q, tail], z_left_in.at[q, tail], right))
        z_send[2, q] = part(left).astype(bf16)
        copies[3, q] = go(ring(3, q, z_send.at[2, q, head], z_right_in.at[q, head], left))
        z_own[q] = part(me_d)

    def pass_on(q):
        copies[0, q].wait_recv()
        z_send[1, q, head] = (z_send[1, q, head].astype(f32) + z_first[0, q].astype(f32)).astype(bf16)
        copies[4, q] = go(ring(4, q, z_send.at[1, q, head], z_left_in.at[q, head], right))
        copies[1, q].wait_recv()
        z_send[2, q, tail] = (z_send[2, q, tail].astype(f32) + z_first[1, q].astype(f32)).astype(bf16)
        copies[5, q] = go(ring(5, q, z_send.at[2, q, tail], z_right_in.at[q, tail], left))

    def finish(q):
        for kind in (2, 3, 4, 5):
            copies[kind, q].wait_recv()
        z = z_own[q] + z_left_in[q].astype(f32) + z_right_in[q].astype(f32)
        sigm = 1.0 / (1.0 + jnp.exp(-z))
        g_cot = got[pl.ds(at_plane[q], rows_plane), pl.ds(dpart, fpart)].astype(f32)
        own_slope[q] = (g_cot * sigm * (1.0 + z * (1.0 - sigm))).astype(bf16)
        at = slopes.at[me_d, pl.ds(at_plane[q], rows_plane)]
        copies[6, q] = go(ring(6, q, own_slope.at[q], at, right))
        copies[7, q] = go(ring(7, q, own_slope.at[q], at, left))
        pltpu.make_async_copy(own_slope.at[q], at, loc_sem.at[5 + q]).start()

    def forward(q):
        copies[6, q].wait_recv()
        at = slopes.at[left, pl.ds(at_plane[q], half)]
        copies[8, q] = go(ring(8, q, at, at, right))
        copies[7, q].wait_recv()
        at = slopes.at[right, pl.ds(at_plane[q] + half, half)]
        copies[9, q] = go(ring(9, q, at, at, left))

    def moments(q):
        kind, piece = divmod(q, pieces)
        source, target = ((m, m_in), (v, v_in))[kind]
        size = target.shape[0] // pieces
        at = pl.ds(piece * size, size)
        copies["swap", q] = swap(1 + kind, source.at[0, at], target.at[at])
        copies["swap", q].start()

    for step, q in order:
        (partials, pass_on, finish, forward, moments)[step](q)

    copies["x"] = pltpu.make_async_copy(got.at[:, pl.ds(0, dpart)], x_out, loc_sem.at[9])
    copies["x"].start()

    for q in range(planes):
        copies[8, q].wait_recv()
        copies[9, q].wait_recv()
        pltpu.make_async_copy(own_slope.at[q], slopes.at[me_d, pl.ds(at_plane[q], rows_plane)], loc_sem.at[5 + q]).wait()
    for copy in pending + exchanged:
        copy.wait_send()
    for d in near_first:
        blocks = slots_plane - 1 if d == 0 else slots_plane
        pltpu.make_async_copy(bytes_of(blocks), bytes_of(blocks), d_send.at[d]).wait()
    copies["x"].wait()
    w_save.wait()
    for kind, target in ((1, m_in), (2, v_in)):
        pltpu.make_async_copy(target, target, swap_recv.at[kind]).wait()
        pltpu.make_async_copy(target, target, swap_send.at[kind]).wait()


def exchange(nd, ne, count, ids, gates, flags, tokens, cot, w, m, v):
    tok_rows, width = tokens.shape
    hidden = cot.shape[1]
    dpart, fpart = width // nd, hidden // nd
    planes = 4
    rows = ne * nd * most
    rows_plane = rows // planes
    half = rows_plane // 2
    top = ids.shape[0]
    vm = pl.BlockSpec(memory_space=pltpu.VMEM)
    hbm = pl.BlockSpec(memory_space=pl.ANY)
    state = jax.ShapeDtypeStruct((dpart, hidden), bf16)
    dma = pltpu.SemaphoreType.DMA
    return pl.pallas_call(
        functools.partial(exchange_kernel, nd, ne, planes),
        out_shape=(
            jax.ShapeDtypeStruct((rows, dpart), bf16),
            jax.ShapeDtypeStruct((nd, rows, fpart), bf16),
            state, state, state,
        ),
        in_specs=[pl.BlockSpec(memory_space=pltpu.SMEM)] + [vm] * 3 + [hbm] * 5,
        out_specs=(hbm,) * 5,
        scratch_shapes=[
            pltpu.VMEM((2 * nd * tok_rows, dpart + fpart), bf16),
            pltpu.VMEM((3 * top, tok_rows), f32),
            pltpu.VMEM((2 * nd, 3 * top, tok_rows), f32),
            pltpu.VMEM((ne // 2, 2 * nd * tok_rows), f32),
            pltpu.VMEM((ne // 2, 2 * nd * tok_rows), f32),
            pltpu.VMEM((rows, dpart + fpart), bf16),
            pltpu.VMEM((rows, dpart + fpart), bf16),
            pltpu.VMEM((dpart, hidden), bf16),
            pltpu.VMEM((dpart, hidden), bf16),
            pltpu.VMEM((3, planes, rows_plane, fpart), bf16),
            pltpu.VMEM((planes, rows_plane, fpart), f32),
            pltpu.VMEM((2, planes, half, fpart), bf16),
            pltpu.VMEM((planes, rows_plane, fpart), bf16),
            pltpu.VMEM((planes, rows_plane, fpart), bf16),
            pltpu.VMEM((planes, rows_plane, fpart), bf16),
            dma((10,)), dma((3,)), dma((3,)), dma((3, 4)), dma((3, 4)),
            dma((2 * nd - 1,)), dma((2 * nd - 1,)), dma((3, 3)), dma((3, 3)),
            dma((planes,)), dma((planes,)), dma((10, planes)), dma((10, planes)),
        ],
        compiler_params=pltpu.CompilerParams(collective_id=0, has_side_effects=True, vmem_limit_bytes=56 << 20),
    )(count, ids, gates, flags, tokens, cot, w, m, v)


def update_kernel(flags, me, x, slopes, w, m, v, m_in, v_in, w_new, m_new, v_new):
    swapped = flags[me[0]] == 1
    nd, _, fpart = slopes.shape
    for r in range(nd):
        cols = pl.ds(r * fpart, fpart)
        grad = lax.dot_general(x[...], slopes[r], (((0,), (0,)), ((), ())), preferred_element_type=f32)
        first = jnp.where(swapped, m_in[:, cols].astype(f32), m[0, :, cols].astype(f32))
        second = jnp.where(swapped, v_in[:, cols].astype(f32), v[0, :, cols].astype(f32))
        first_new = beta_first * first + (1.0 - beta_first) * grad
        second_new = beta_second * second + (1.0 - beta_second) * grad * grad
        ratio = first_new * (1.0 / bias_first) / (jnp.sqrt(second_new * (1.0 / bias_second)) + epsilon)
        w_new[0, :, cols] = (w[:, cols].astype(f32) - learn_rate * ratio).astype(bf16)
        m_new[0, :, cols] = first_new.astype(bf16)
        v_new[0, :, cols] = second_new.astype(bf16)


def update(flags, me, x, slopes, w, m, v, m_in, v_in):
    rows, dpart = x.shape
    nd, _, fpart = slopes.shape
    hidden = nd * fpart
    block = 128
    state = jax.ShapeDtypeStruct((1, dpart, hidden), bf16)
    here = pl.BlockSpec((1, block, hidden), lambda i, flags, me: (0, i, 0))
    stays = pl.BlockSpec((1, block, hidden), lambda i, flags, me: (0, i * (1 - flags[me[0]]), 0))
    moved = pl.BlockSpec((block, hidden), lambda i, flags, me: (i * flags[me[0]], 0))
    return pl.pallas_call(
        update_kernel,
        out_shape=(state, state, state),
        grid_spec=pltpu.PrefetchScalarGridSpec(
            num_scalar_prefetch=2,
            grid=(dpart // block,),
            in_specs=[
                pl.BlockSpec((rows, block), lambda i, flags, me: (0, i)),
                pl.BlockSpec((nd, rows, fpart), lambda i, flags, me: (0, 0, 0)),
                pl.BlockSpec((block, hidden), lambda i, flags, me: (i, 0)),
                stays, stays, moved, moved,
            ],
            out_specs=(here, here, here),
        ),
        compiler_params=pltpu.CompilerParams(vmem_limit_bytes=60 << 20),
    )(flags, me, x, slopes, w, m, v, m_in, v_in)


def shards(tokens, cotangent, expert_ids, gate_values, counts, swap_flags, weights, first_moment, second_moment):
    ne, nd = lax.axis_size("expert"), lax.axis_size("dp")
    x, slopes, w_in, m_in, v_in = exchange(
        nd, ne, counts, expert_ids.T, gate_values.T, swap_flags[None], tokens, cotangent, weights, first_moment, second_moment
    )
    me = lax.axis_index("expert").astype(i32)[None]
    return update(swap_flags, me, x, slopes, w_in, first_moment, second_moment, m_in, v_in)


def solution(mesh):
    placed = (
        P(("dp", "expert"), None),
        P(("dp", "expert"), None),
        P(("dp", "expert"), None),
        P(("dp", "expert"), None),
        P(("dp", "expert")),
        P(),
        P("expert", "dp", None),
        P("expert", "dp", None),
        P("expert", "dp", None),
    )
    return jax.shard_map(
        shards,
        mesh=mesh,
        in_specs=placed,
        out_specs=(P("expert", "dp", None), P("expert", "dp", None), P("expert", "dp", None)),
        check_vma=False,
    )
```

```python
import functools

import jax
import jax.numpy as jnp
from jax import lax
from jax.experimental import pallas as pl
from jax.experimental.pallas import tpu as pltpu
from jax.sharding import PartitionSpec as P

beta_first = 0.9
beta_second = 0.95
bias_first = 1.0 - 0.9**3
bias_second = 1.0 - 0.95**3
learn_rate = 0.005
epsilon = 1e-08
most = 6
f32, bf16, i32 = jnp.float32, jnp.bfloat16, jnp.int32
MESH = pl.DeviceIdType.MESH
near_first = (0, 1, 3, 2)
pieces = ((0, 0, 256), (0, 256, 640), (1, 0, 896))
PART, PASS, FINISH, FORWARD, MOMENTS, GRAD, PICK = range(7)
order = (
    (PICK, 0), (PICK, 1), (PICK, 2), (PART, 0), (PICK, 3), (PASS, 0), (PART, 1), (PASS, 1), (PART, 2), (MOMENTS, 1), (MOMENTS, 2), (FINISH, 0), (PASS, 2), (FINISH, 1), (FORWARD, 0), (PART, 3), (FORWARD, 1), (FINISH, 2), (PASS, 3), (GRAD, 0), (FORWARD, 2), (FINISH, 3), (GRAD, 1), (FORWARD, 3), (GRAD, 2),
)


def exchange_kernel(
    nd, ne, planes,
    count, ids, gates, flags, tokens, cot, w, m, v,
    x_last, s_last, g_out, w_in, m_in, v_in,
    rx, aux, aux_in, places, weights, send, got, w_own, w_mov, z_send, z_own, z_first, z_right_in, z_left_in, slopes, g_sum,
    loc_sem, swap_send, swap_recv, ex_send, ex_recv, a_send, a_recv, f_send, f_recv, d_send, d_recv, r_send, r_recv,
):
    me_d, me_e = lax.axis_index("dp"), lax.axis_index("expert")
    right, left, opp = lax.rem(me_d + 1, nd), lax.rem(me_d + nd - 1, nd), lax.rem(me_d + 2, nd)
    mate = lax.rem(me_e + ne // 2, ne)
    top, tok_rows = ids.shape
    dpart, fpart = tokens.shape[1] // nd, cot.shape[1] // nd
    my_z = lax.rem(me_e // 2, 2)
    pair = me_e + 2 - 4 * my_z
    here = (me_e // 4) * 2 + lax.rem(me_e, 2)
    nh = ne // 2
    sources = 2 * nd
    per_slot = sources * most
    slots_plane = nh // planes
    my_plane = here // slots_plane

    def expert_at(spot):
        return (spot // 2) * 4 + 2 * my_z + lax.rem(spot, 2)

    rows_plane = slots_plane * per_slot
    half = rows_plane // 2

    barrier = pltpu.get_barrier_semaphore()

    def greet(i, carry):
        spot = lax.rem(here + i, nh)
        pl.semaphore_signal(barrier, inc=1, device_id={"expert": expert_at(spot)}, device_id_type=MESH)
        return carry

    lax.fori_loop(1, nh, greet, 0)
    others = [(i, e) for i in range(nd) for e in (me_e, pair)][1:]
    for i, e in others:
        pl.semaphore_signal(barrier, inc=1, device_id={"dp": lax.rem(me_d + i, nd), "expert": e}, device_id_type=MESH)
    pl.semaphore_wait(barrier, nh - 1 + len(others))

    def swap(kind, src, dst):
        return pltpu.make_async_remote_copy(
            src_ref=src, dst_ref=dst, send_sem=swap_send.at[kind], recv_sem=swap_recv.at[kind],
            device_id={"expert": mate}, device_id_type=MESH,
        )

    w_swap = swap(0, w.at[0], w_mov)

    def remote(src, dst, send_sem, recv_sem, dp, expert):
        return pltpu.make_async_remote_copy(
            src_ref=src, dst_ref=dst, send_sem=send_sem, recv_sem=recv_sem,
            device_id={"dp": dp, "expert": expert}, device_id_type=MESH,
        )

    def rows_from(dp, z):
        return pl.ds(pl.multiple_of((z * nd + dp) * tok_rows, tok_rows), tok_rows)

    my_rows = rows_from(me_d, my_z)
    side = lax.rem(me_d + nd - 1 + 2 * my_z, nd)

    def tok_cols(r):
        return pl.ds(pl.multiple_of(r * dpart, 128), dpart)

    def cot_cols(r):
        return pl.ds(pl.multiple_of(r * fpart, 128), fpart)

    exchanged = []
    low, high = me_e - 2 * my_z, me_e - 2 * my_z + 2
    split = tok_rows // 2
    parts = ((0, split, 0, dpart), (split, split, 0, dpart), (0, tok_rows, dpart, fpart))

    def part_of(kind, first):
        row, height, col, wide = parts[kind]
        return rx.at[pl.ds(pl.multiple_of(first + row, split), height), pl.ds(col, wide)]

    def first_row(dp, z):
        return (z * nd + dp) * tok_rows

    for kind, (row, height, col, wide) in enumerate(parts):
        for way, (dp, expert, number) in enumerate(
            ((opp, pair, 2), (right, low, my_z), (left, high, my_z), (me_d, pair, 3))
        ):
            src = tokens.at[pl.ds(row, height), tok_cols(dp)] if col == 0 else cot.at[:, cot_cols(dp)]
            dst = part_of(kind, first_row(me_d, my_z))
            copy = remote(src, dst, ex_send.at[kind, way], ex_recv.at[kind, number], dp, expert)
            copy.start()
            exchanged.append(copy)
    def moments(q):
        kind, first, height = pieces[q]
        source, target = ((m, m_in), (v, v_in))[kind]
        at = pl.ds(first, height)
        swap(1 + kind, source.at[0, at], target.at[at]).start()

    w_swap.start()
    moments(0)
    own_x = pltpu.make_async_copy(tokens.at[:, tok_cols(me_d)], rx.at[my_rows, pl.ds(0, dpart)], loc_sem.at[0])
    own_c = pltpu.make_async_copy(cot.at[:, cot_cols(me_d)], rx.at[my_rows, pl.ds(dpart, fpart)], loc_sem.at[1])
    own_w = pltpu.make_async_copy(w.at[0], w_own, loc_sem.at[2])
    own_x.start()
    own_c.start()
    own_w.start()

    experts_col = lax.broadcasted_iota(i32, (ne, tok_rows), 0)
    live = lax.broadcasted_iota(i32, (ne, tok_rows), 1) < count[0]
    every = jnp.zeros((ne, tok_rows), f32)
    for k in range(top):
        every = every + jnp.where((ids[pl.ds(k, 1), :] == experts_col) & live, 1.0, 0.0)
    earlier = jnp.where(
        lax.broadcasted_iota(i32, (tok_rows, tok_rows), 0) < lax.broadcasted_iota(i32, (tok_rows, tok_rows), 1), 1.0, 0.0
    )
    ranked = jnp.dot(every.astype(bf16), earlier.astype(bf16), preferred_element_type=f32)
    flag_row = jnp.broadcast_to(flags[...], (ne, ne))
    expert_row = lax.broadcasted_iota(i32, (ne, ne), 0)
    flag_col = jnp.sum(jnp.where(expert_row == lax.broadcasted_iota(i32, (ne, ne), 1), flag_row, 0), axis=1, keepdims=True)
    expert_col = lax.broadcasted_iota(i32, (ne, 1), 0)
    slot_col = jnp.where(flag_col == 1, lax.rem(expert_col + ne // 2, ne), expert_col).astype(f32) + 1.0
    for k in range(top):
        hit = (ids[pl.ds(k, 1), :] == experts_col) & live
        slot = jnp.sum(jnp.where(hit, slot_col, 0.0), axis=0, keepdims=True)
        rank = jnp.sum(jnp.where(hit, ranked, 0.0), axis=0, keepdims=True)
        aux[pl.ds(k, 1), :] = slot - 1.0
        aux[pl.ds(top + k, 1), :] = rank + ((my_z * nd + me_d) * most + 1)
    aux[pl.ds(2 * top, top), :] = gates[...]
    my_source = my_z * nd + me_d
    aux_in[my_source] = aux[...]
    for n, (i, e) in enumerate(others):
        copy = remote(aux, aux_in.at[my_source], a_send.at[n], a_recv.at[n], lax.rem(me_d + i, nd), e)
        copy.start()
        exchanged.append(copy)

    for kind in range(len(parts)):
        for number, dp, z in ((1 - my_z, side, 1 - my_z), (my_z, side, my_z), (2, opp, 1 - my_z)):
            at = part_of(kind, first_row(dp, z))
            pltpu.make_async_copy(at, at, ex_recv.at[kind, number]).wait()
            copy = remote(at, at, f_send.at[kind, number], f_recv.at[kind, number], me_d, pair)
            copy.start()
            exchanged.append(copy)
    own_w.wait()
    w_swap.wait()
    steps = 7
    w_rows = w_own.shape[0] // steps

    mine = lax.broadcasted_iota(i32, (1, ne), 1) == me_e
    own_flag = jnp.sum(jnp.where(mine, flags[...], 0), axis=1, keepdims=True)

    def choose(i, carry):
        at = pl.ds(pl.multiple_of(i * w_rows, w_rows), w_rows)
        w_own[at] = jnp.where(own_flag == 1, w_mov[at].astype(f32), w_own[at].astype(f32)).astype(bf16)
        return carry

    lax.fori_loop(0, steps, choose, 0)
    w_save = pltpu.make_async_copy(w_own, w_in, loc_sem.at[4])
    w_save.start()

    own_x.wait()
    own_c.wait()
    for kind in range(len(parts)):
        at = part_of(kind, 0)
        pltpu.make_async_copy(at, at, ex_recv.at[kind, 3]).wait()
        for number in range(3):
            pltpu.make_async_copy(at, at, f_recv.at[kind, number]).wait()
    for n in range(len(others)):
        pltpu.make_async_copy(aux, aux, a_recv.at[n]).wait()

    lanes = sources * tok_rows
    to_slot, to_row, gate = (
        jnp.concatenate([aux_in[g, pl.ds(part * top, top), :] for g in range(sources)], axis=1) for part in range(3)
    )
    slots = expert_at(lax.broadcasted_iota(i32, (nh, lanes), 0)).astype(f32)
    place = jnp.zeros((nh, lanes), f32)
    scale = jnp.zeros((nh, lanes), f32)
    for k in range(top):
        hit = slots == to_slot[k : k + 1]
        place = jnp.where(hit, to_row[k : k + 1], place)
        scale = jnp.where(hit, gate[k : k + 1], scale)
    places[...] = place
    weights[...] = scale
    my_at = pl.ds(pl.multiple_of(here * per_slot, per_slot), per_slot)

    def rows_of(slot):
        return pl.ds(pl.multiple_of(slot * per_slot, per_slot), per_slot)

    picked = (slots_plane, per_slot, lanes)
    number = (lax.broadcasted_iota(i32, picked, 1) + 1).astype(f32)
    own_rows = pltpu.make_async_copy(send.at[my_at], got.at[my_at], loc_sem.at[3])

    def pick(q):
        d = near_first[q]
        plane = lax.rem(my_plane + d, planes)
        plane_slots = pl.ds(pl.multiple_of(plane * slots_plane, slots_plane), slots_plane)
        hit = jnp.broadcast_to(places[plane_slots, :][:, None, :], picked) == number
        picker = jnp.where(hit, 1.0, 0.0).astype(bf16).reshape(rows_plane, lanes)
        gated = jnp.where(hit, jnp.broadcast_to(weights[plane_slots, :][:, None, :], picked), 0.0)
        gated = gated.astype(bf16).reshape(rows_plane, lanes)
        plane_rows = pl.ds(pl.multiple_of(plane * rows_plane, rows_plane), rows_plane)
        xs = jnp.dot(picker, rx[:, pl.ds(0, dpart)], preferred_element_type=f32)
        cs = jnp.dot(gated, rx[:, pl.ds(dpart, fpart)], preferred_element_type=f32)
        send[plane_rows, pl.ds(0, dpart)] = xs.astype(bf16)
        send[plane_rows, pl.ds(dpart, fpart)] = cs.astype(bf16)

        def dispatch(step, carry):
            slot = plane * slots_plane + lax.rem(here + step, slots_plane)
            pltpu.make_async_remote_copy(
                src_ref=send.at[rows_of(slot)], dst_ref=got.at[my_at],
                send_sem=d_send.at[d], recv_sem=d_recv.at[d],
                device_id={"expert": expert_at(slot)}, device_id_type=MESH,
            ).start()
            return carry

        lax.fori_loop(1 if d == 0 else 0, slots_plane, dispatch, 0)
        if d == 0:
            own_rows.start()

    def ring(kind, q, src, dst, to):
        return pltpu.make_async_remote_copy(
            src_ref=src, dst_ref=dst, send_sem=r_send.at[kind, q], recv_sem=r_recv.at[kind, q],
            device_id={"dp": to}, device_id_type=MESH,
        )

    head, tail = pl.ds(0, half), pl.ds(half, half)
    at_plane = [
        pl.multiple_of(lax.rem(my_plane + planes - d, planes) * rows_plane, rows_plane) for d in near_first
    ]
    pending, settled = [], []

    def go(copy):
        copy.start()
        pending.append(copy)
        return copy

    copies = {}

    def bytes_of(blocks):
        return got.at[pl.ds(0, blocks * per_slot)]

    def partials(q):
        d = near_first[q]
        blocks = slots_plane - 1 if d == 0 else slots_plane
        pltpu.make_async_copy(bytes_of(blocks), bytes_of(blocks), d_recv.at[d]).wait()
        if d == 0:
            own_rows.wait()
        if q == planes - 1:
            rows_out = got.at[pl.ds(at_plane[q], rows_plane), pl.ds(0, dpart)]
            copies["x"] = pltpu.make_async_copy(rows_out, x_last, loc_sem.at[6])
            copies["x"].start()
        x = got[pl.ds(at_plane[q], rows_plane), pl.ds(0, dpart)]

        def part(r):
            cols = pl.ds(pl.multiple_of(r * fpart, 128), fpart)
            return jnp.dot(x, w_own[:, cols], preferred_element_type=f32)

        z_send[0, q] = part(opp).astype(bf16)
        copies[0, q] = go(ring(0, q, z_send.at[0, q, head], z_first.at[0, q], right))
        copies[1, q] = go(ring(1, q, z_send.at[0, q, tail], z_first.at[1, q], left))
        z_send[1, q] = part(right).astype(bf16)
        copies[2, q] = go(ring(2, q, z_send.at[1, q, tail], z_left_in.at[q, tail], right))
        z_send[2, q] = part(left).astype(bf16)
        copies[3, q] = go(ring(3, q, z_send.at[2, q, head], z_right_in.at[q, head], left))
        z_own[q] = part(me_d)

    def pass_on(q):
        copies[0, q].wait_recv()
        z_send[1, q, head] = (z_send[1, q, head].astype(f32) + z_first[0, q].astype(f32)).astype(bf16)
        copies[4, q] = go(ring(4, q, z_send.at[1, q, head], z_left_in.at[q, head], right))
        copies[1, q].wait_recv()
        z_send[2, q, tail] = (z_send[2, q, tail].astype(f32) + z_first[1, q].astype(f32)).astype(bf16)
        copies[5, q] = go(ring(5, q, z_send.at[2, q, tail], z_right_in.at[q, tail], left))

    def finish(q):
        for kind in (2, 3, 4, 5):
            copies[kind, q].wait_recv()
        z = z_own[q] + z_left_in[q].astype(f32) + z_right_in[q].astype(f32)
        sigm = 1.0 / (1.0 + jnp.exp(-z))
        g_cot = got[pl.ds(at_plane[q], rows_plane), pl.ds(dpart, fpart)].astype(f32)
        slope = (g_cot * sigm * (1.0 + z * (1.0 - sigm))).astype(bf16)
        if q < planes - 1:
            slopes[q, me_d] = slope
            src = slopes.at[q, me_d]
        else:
            for kind in (0, 1):
                copies[kind, q].wait_send()
                settled.append(copies[kind, q])
            z_send[0, q] = slope
            src = z_send.at[0, q]
            copies["s"] = pltpu.make_async_copy(src, s_last.at[me_d], loc_sem.at[5])
            copies["s"].start()
        at = block_of(q, me_d, 0, rows_plane)
        copies[6, q] = go(ring(6, q, src, at, right))
        copies[7, q] = go(ring(7, q, src, at, left))

    def block_of(q, dp, first, height):
        held = slopes.at[q] if q < planes - 1 else s_last
        return held.at[dp, pl.ds(first, height)]

    def forward(q):
        copies[6, q].wait_recv()
        at = block_of(q, left, 0, half)
        copies[8, q] = go(ring(8, q, at, at, right))
        copies[7, q].wait_recv()
        at = block_of(q, right, half, half)
        copies[9, q] = go(ring(9, q, at, at, left))

    def gradient(q):
        copies[8, q].wait_recv()
        copies[9, q].wait_recv()
        x = got[pl.ds(at_plane[q], rows_plane), pl.ds(0, dpart)]
        for r in range(nd):
            cols = pl.ds(r * fpart, fpart)
            more = lax.dot_general(x, slopes[q, r], (((0,), (0,)), ((), ())), preferred_element_type=f32)
            if q == 0:
                g_sum[:, cols] = more
            else:
                g_sum[:, cols] = g_sum[:, cols] + more

    for step, q in order:
        (partials, pass_on, finish, forward, moments, gradient, pick)[step](q)

    g_save = pltpu.make_async_copy(g_sum, g_out, loc_sem.at[7])
    g_save.start()

    copies[8, planes - 1].wait_recv()
    copies[9, planes - 1].wait_recv()
    for copy in pending + exchanged:
        if not any(copy is other for other in settled):
            copy.wait_send()
    for d in near_first:
        blocks = slots_plane - 1 if d == 0 else slots_plane
        pltpu.make_async_copy(bytes_of(blocks), bytes_of(blocks), d_send.at[d]).wait()
    copies["x"].wait()
    copies["s"].wait()
    g_save.wait()
    w_save.wait()
    for kind, target in ((1, m_in), (2, v_in)):
        pltpu.make_async_copy(target, target, swap_recv.at[kind]).wait()
        pltpu.make_async_copy(target, target, swap_send.at[kind]).wait()


def exchange(nd, ne, count, ids, gates, flags, tokens, cot, w, m, v):
    tok_rows, width = tokens.shape
    hidden = cot.shape[1]
    dpart, fpart = width // nd, hidden // nd
    planes = 4
    rows = ne * nd * most
    rows_plane = rows // planes
    half = rows_plane // 2
    top = ids.shape[0]
    vm = pl.BlockSpec(memory_space=pltpu.VMEM)
    hbm = pl.BlockSpec(memory_space=pl.ANY)
    state = jax.ShapeDtypeStruct((dpart, hidden), bf16)
    dma = pltpu.SemaphoreType.DMA
    return pl.pallas_call(
        functools.partial(exchange_kernel, nd, ne, planes),
        out_shape=(
            jax.ShapeDtypeStruct((rows_plane, dpart), bf16),
            jax.ShapeDtypeStruct((nd, rows_plane, fpart), bf16),
            jax.ShapeDtypeStruct((dpart, hidden), f32),
            state, state, state,
        ),
        in_specs=[pl.BlockSpec(memory_space=pltpu.SMEM)] + [vm] * 3 + [hbm] * 5,
        out_specs=(hbm,) * 6,
        scratch_shapes=[
            pltpu.VMEM((2 * nd * tok_rows, dpart + fpart), bf16),
            pltpu.VMEM((3 * top, tok_rows), f32),
            pltpu.VMEM((2 * nd, 3 * top, tok_rows), f32),
            pltpu.VMEM((ne // 2, 2 * nd * tok_rows), f32),
            pltpu.VMEM((ne // 2, 2 * nd * tok_rows), f32),
            pltpu.VMEM((rows, dpart + fpart), bf16),
            pltpu.VMEM((rows, dpart + fpart), bf16),
            pltpu.VMEM((dpart, hidden), bf16),
            pltpu.VMEM((dpart, hidden), bf16),
            pltpu.VMEM((3, planes, rows_plane, fpart), bf16),
            pltpu.VMEM((planes, rows_plane, fpart), f32),
            pltpu.VMEM((2, planes, half, fpart), bf16),
            pltpu.VMEM((planes, rows_plane, fpart), bf16),
            pltpu.VMEM((planes, rows_plane, fpart), bf16),
            pltpu.VMEM((planes - 1, nd, rows_plane, fpart), bf16),
            pltpu.VMEM((dpart, hidden), f32),
            dma((10,)), dma((3,)), dma((3,)), dma((3, 4)), dma((3, 4)),
            dma((2 * nd - 1,)), dma((2 * nd - 1,)), dma((3, 3)), dma((3, 3)),
            dma((planes,)), dma((planes,)), dma((10, planes)), dma((10, planes)),
        ],
        compiler_params=pltpu.CompilerParams(collective_id=0, has_side_effects=True, vmem_limit_bytes=56 << 20),
    )(count, ids, gates, flags, tokens, cot, w, m, v)


def update_kernel(flags, me, x, slopes, g, w, m, v, m_in, v_in, w_new, m_new, v_new):
    swapped = flags[me[0]] == 1
    nd, _, fpart = slopes.shape

    def step(first_of, second_of):
        for r in range(nd):
            cols = pl.ds(r * fpart, fpart)
            last = lax.dot_general(x[...], slopes[r], (((0,), (0,)), ((), ())), preferred_element_type=f32)
            grad = g[:, cols] + last
            first_new = beta_first * first_of(cols).astype(f32) + (1.0 - beta_first) * grad
            second_new = beta_second * second_of(cols).astype(f32) + (1.0 - beta_second) * grad * grad
            scaled = second_new * (1.0 / bias_second)
            ratio = first_new * (learn_rate / bias_first) / (scaled * lax.rsqrt(scaled) + epsilon)
            w_new[0, :, cols] = (w[:, cols].astype(f32) - ratio).astype(bf16)
            m_new[0, :, cols] = first_new.astype(bf16)
            v_new[0, :, cols] = second_new.astype(bf16)

    @pl.when(swapped)
    def _():
        step(lambda cols: m_in[:, cols], lambda cols: v_in[:, cols])

    @pl.when(jnp.logical_not(swapped))
    def _():
        step(lambda cols: m[0, :, cols], lambda cols: v[0, :, cols])


def update(flags, me, x, slopes, g, w, m, v, m_in, v_in):
    rows, dpart = x.shape
    nd, _, fpart = slopes.shape
    hidden = nd * fpart
    block = 128
    state = jax.ShapeDtypeStruct((1, dpart, hidden), bf16)
    here = pl.BlockSpec((1, block, hidden), lambda i, flags, me: (0, i, 0))
    stays = pl.BlockSpec((1, block, hidden), lambda i, flags, me: (0, i * (1 - flags[me[0]]), 0))
    moved = pl.BlockSpec((block, hidden), lambda i, flags, me: (i * flags[me[0]], 0))
    return pl.pallas_call(
        update_kernel,
        out_shape=(state, state, state),
        grid_spec=pltpu.PrefetchScalarGridSpec(
            num_scalar_prefetch=2,
            grid=(dpart // block,),
            in_specs=[
                pl.BlockSpec((rows, block), lambda i, flags, me: (0, i)),
                pl.BlockSpec((nd, rows, fpart), lambda i, flags, me: (0, 0, 0)),
                pl.BlockSpec((block, hidden), lambda i, flags, me: (i, 0)),
                pl.BlockSpec((block, hidden), lambda i, flags, me: (i, 0)),
                stays, stays, moved, moved,
            ],
            out_specs=(here, here, here),
        ),
        compiler_params=pltpu.CompilerParams(vmem_limit_bytes=60 << 20),
    )(flags, me, x, slopes, g, w, m, v, m_in, v_in)


def shards(tokens, cotangent, expert_ids, gate_values, counts, swap_flags, weights, first_moment, second_moment):
    ne, nd = lax.axis_size("expert"), lax.axis_size("dp")
    x, slopes, g, w_in, m_in, v_in = exchange(
        nd, ne, counts, expert_ids.T, gate_values.T, swap_flags[None], tokens, cotangent, weights, first_moment, second_moment
    )
    me = lax.axis_index("expert").astype(i32)[None]
    return update(swap_flags, me, x, slopes, g, w_in, first_moment, second_moment, m_in, v_in)


def solution(mesh):
    placed = (
        P(("dp", "expert"), None),
        P(("dp", "expert"), None),
        P(("dp", "expert"), None),
        P(("dp", "expert"), None),
        P(("dp", "expert")),
        P(),
        P("expert", "dp", None),
        P("expert", "dp", None),
        P("expert", "dp", None),
    )
    return jax.shard_map(
        shards,
        mesh=mesh,
        in_specs=placed,
        out_specs=(P("expert", "dp", None), P("expert", "dp", None), P("expert", "dp", None)),
        check_vma=False,
    )
```

```python
import functools

import jax
import jax.numpy as jnp
from jax import lax
from jax.experimental import pallas as pl
from jax.experimental.pallas import tpu as pltpu
from jax.sharding import PartitionSpec as P

beta_first = 0.9
beta_second = 0.95
bias_first = 1.0 - 0.9**3
bias_second = 1.0 - 0.95**3
learn_rate = 0.005
epsilon = 1e-08
most = 6
f32, bf16, i32 = jnp.float32, jnp.bfloat16, jnp.int32
MESH = pl.DeviceIdType.MESH
near_first = (0, 1, 3, 2)
pieces = ((0, 0, 256), (0, 256, 640), (1, 0, 896))
PART, PASS, FINISH, FORWARD, MOMENTS, GRAD, PICK = range(7)
order = (
    (PICK, 0), (PICK, 1), (PICK, 2), (PART, 0), (PICK, 3), (PASS, 0), (FINISH, 0), (PART, 1), (PASS, 1), (PART, 2), (MOMENTS, 1), (MOMENTS, 2), (FORWARD, 0), (PASS, 2), (FINISH, 1), (PART, 3), (PASS, 3), (FORWARD, 1), (FINISH, 2), (GRAD, 0), (FORWARD, 2), (FINISH, 3), (GRAD, 1), (FORWARD, 3), (GRAD, 2),
)


def exchange_kernel(
    nd, ne, planes,
    count, ids, gates, flags, tokens, cot, w, m, v,
    x_last, s_last, g_out, w_in, m_in, v_in,
    rx, aux, aux_in, places, weights, send, got, w_own, w_mov, z_send, z_own, z_first, z_right_in, z_left_in, slopes, g_sum,
    loc_sem, swap_send, swap_recv, ex_send, ex_recv, a_send, a_recv, f_send, f_recv, d_send, d_recv, r_send, r_recv,
):
    me_d, me_e = lax.axis_index("dp"), lax.axis_index("expert")
    right, left, opp = lax.rem(me_d + 1, nd), lax.rem(me_d + nd - 1, nd), lax.rem(me_d + 2, nd)
    mate = lax.rem(me_e + ne // 2, ne)
    top, tok_rows = ids.shape
    dpart, fpart = tokens.shape[1] // nd, cot.shape[1] // nd
    my_z = lax.rem(me_e // 2, 2)
    pair = me_e + 2 - 4 * my_z
    here = (me_e // 4) * 2 + lax.rem(me_e, 2)
    nh = ne // 2
    sources = 2 * nd
    per_slot = sources * most
    slots_plane = nh // planes
    my_plane = here // slots_plane

    def expert_at(spot):
        return (spot // 2) * 4 + 2 * my_z + lax.rem(spot, 2)

    rows_plane = slots_plane * per_slot
    half = rows_plane // 2

    barrier = pltpu.get_barrier_semaphore()

    def greet(i, carry):
        spot = lax.rem(here + i, nh)
        pl.semaphore_signal(barrier, inc=1, device_id={"expert": expert_at(spot)}, device_id_type=MESH)
        return carry

    lax.fori_loop(1, nh, greet, 0)
    others = [(i, e) for i in range(nd) for e in (me_e, pair)][1:]
    for i, e in others:
        pl.semaphore_signal(barrier, inc=1, device_id={"dp": lax.rem(me_d + i, nd), "expert": e}, device_id_type=MESH)
    pl.semaphore_wait(barrier, nh - 1 + len(others))

    def swap(kind, src, dst):
        return pltpu.make_async_remote_copy(
            src_ref=src, dst_ref=dst, send_sem=swap_send.at[kind], recv_sem=swap_recv.at[kind],
            device_id={"expert": mate}, device_id_type=MESH,
        )

    w_swap = swap(0, w.at[0], w_mov)

    def remote(src, dst, send_sem, recv_sem, dp, expert):
        return pltpu.make_async_remote_copy(
            src_ref=src, dst_ref=dst, send_sem=send_sem, recv_sem=recv_sem,
            device_id={"dp": dp, "expert": expert}, device_id_type=MESH,
        )

    def rows_from(dp, z):
        return pl.ds(pl.multiple_of((z * nd + dp) * tok_rows, tok_rows), tok_rows)

    my_rows = rows_from(me_d, my_z)
    side = lax.rem(me_d + nd - 1 + 2 * my_z, nd)

    def tok_cols(r):
        return pl.ds(pl.multiple_of(r * dpart, 128), dpart)

    def cot_cols(r):
        return pl.ds(pl.multiple_of(r * fpart, 128), fpart)

    exchanged = []
    low, high = me_e - 2 * my_z, me_e - 2 * my_z + 2
    split = tok_rows // 2
    parts = ((0, split, 0, dpart), (split, split, 0, dpart), (0, tok_rows, dpart, fpart))

    def part_of(kind, first):
        row, height, col, wide = parts[kind]
        return rx.at[pl.ds(pl.multiple_of(first + row, split), height), pl.ds(col, wide)]

    def first_row(dp, z):
        return (z * nd + dp) * tok_rows

    for kind, (row, height, col, wide) in enumerate(parts):
        for way, (dp, expert, number) in enumerate(
            ((opp, pair, 2), (right, low, my_z), (left, high, my_z), (me_d, pair, 3))
        ):
            src = tokens.at[pl.ds(row, height), tok_cols(dp)] if col == 0 else cot.at[:, cot_cols(dp)]
            dst = part_of(kind, first_row(me_d, my_z))
            copy = remote(src, dst, ex_send.at[kind, way], ex_recv.at[kind, number], dp, expert)
            copy.start()
            exchanged.append(copy)
    def moments(q):
        kind, first, height = pieces[q]
        source, target = ((m, m_in), (v, v_in))[kind]
        at = pl.ds(first, height)
        swap(1 + kind, source.at[0, at], target.at[at]).start()

    w_swap.start()
    moments(0)
    own_x = pltpu.make_async_copy(tokens.at[:, tok_cols(me_d)], rx.at[my_rows, pl.ds(0, dpart)], loc_sem.at[0])
    own_c = pltpu.make_async_copy(cot.at[:, cot_cols(me_d)], rx.at[my_rows, pl.ds(dpart, fpart)], loc_sem.at[1])
    own_w = pltpu.make_async_copy(w.at[0], w_own, loc_sem.at[2])
    own_x.start()
    own_c.start()
    own_w.start()

    experts_col = lax.broadcasted_iota(i32, (ne, tok_rows), 0)
    live = lax.broadcasted_iota(i32, (ne, tok_rows), 1) < count[0]
    every = jnp.zeros((ne, tok_rows), f32)
    for k in range(top):
        every = every + jnp.where((ids[pl.ds(k, 1), :] == experts_col) & live, 1.0, 0.0)
    earlier = jnp.where(
        lax.broadcasted_iota(i32, (tok_rows, tok_rows), 0) < lax.broadcasted_iota(i32, (tok_rows, tok_rows), 1), 1.0, 0.0
    )
    ranked = jnp.dot(every.astype(bf16), earlier.astype(bf16), preferred_element_type=f32)
    flag_row = jnp.broadcast_to(flags[...], (ne, ne))
    expert_row = lax.broadcasted_iota(i32, (ne, ne), 0)
    flag_col = jnp.sum(jnp.where(expert_row == lax.broadcasted_iota(i32, (ne, ne), 1), flag_row, 0), axis=1, keepdims=True)
    expert_col = lax.broadcasted_iota(i32, (ne, 1), 0)
    slot_col = jnp.where(flag_col == 1, lax.rem(expert_col + ne // 2, ne), expert_col).astype(f32) + 1.0
    for k in range(top):
        hit = (ids[pl.ds(k, 1), :] == experts_col) & live
        slot = jnp.sum(jnp.where(hit, slot_col, 0.0), axis=0, keepdims=True)
        rank = jnp.sum(jnp.where(hit, ranked, 0.0), axis=0, keepdims=True)
        aux[pl.ds(k, 1), :] = slot - 1.0
        aux[pl.ds(top + k, 1), :] = rank + ((my_z * nd + me_d) * most + 1)
    aux[pl.ds(2 * top, top), :] = gates[...]
    my_source = my_z * nd + me_d
    aux_in[my_source] = aux[...]
    for n, (i, e) in enumerate(others):
        copy = remote(aux, aux_in.at[my_source], a_send.at[n], a_recv.at[n], lax.rem(me_d + i, nd), e)
        copy.start()
        exchanged.append(copy)

    for kind in range(len(parts)):
        for number, dp, z in ((1 - my_z, side, 1 - my_z), (my_z, side, my_z), (2, opp, 1 - my_z)):
            at = part_of(kind, first_row(dp, z))
            pltpu.make_async_copy(at, at, ex_recv.at[kind, number]).wait()
            copy = remote(at, at, f_send.at[kind, number], f_recv.at[kind, number], me_d, pair)
            copy.start()
            exchanged.append(copy)
    own_w.wait()
    w_swap.wait()
    steps = 7
    w_rows = w_own.shape[0] // steps

    mine = lax.broadcasted_iota(i32, (1, ne), 1) == me_e
    own_flag = jnp.sum(jnp.where(mine, flags[...], 0), axis=1, keepdims=True)

    def choose(i, carry):
        at = pl.ds(pl.multiple_of(i * w_rows, w_rows), w_rows)
        w_own[at] = jnp.where(own_flag == 1, w_mov[at].astype(f32), w_own[at].astype(f32)).astype(bf16)
        return carry

    lax.fori_loop(0, steps, choose, 0)
    w_save = pltpu.make_async_copy(w_own, w_in, loc_sem.at[4])
    w_save.start()

    own_x.wait()
    own_c.wait()
    for kind in range(len(parts)):
        at = part_of(kind, 0)
        pltpu.make_async_copy(at, at, ex_recv.at[kind, 3]).wait()
        for number in range(3):
            pltpu.make_async_copy(at, at, f_recv.at[kind, number]).wait()
    for n in range(len(others)):
        pltpu.make_async_copy(aux, aux, a_recv.at[n]).wait()

    lanes = sources * tok_rows
    to_slot, to_row, gate = (
        jnp.concatenate([aux_in[g, pl.ds(part * top, top), :] for g in range(sources)], axis=1) for part in range(3)
    )
    slots = expert_at(lax.broadcasted_iota(i32, (nh, lanes), 0)).astype(f32)
    place = jnp.zeros((nh, lanes), f32)
    scale = jnp.zeros((nh, lanes), f32)
    for k in range(top):
        hit = slots == to_slot[k : k + 1]
        place = jnp.where(hit, to_row[k : k + 1], place)
        scale = jnp.where(hit, gate[k : k + 1], scale)
    places[...] = place
    weights[...] = scale
    my_at = pl.ds(pl.multiple_of(here * per_slot, per_slot), per_slot)

    def rows_of(slot):
        return pl.ds(pl.multiple_of(slot * per_slot, per_slot), per_slot)

    picked = (slots_plane, per_slot, lanes)
    number = (lax.broadcasted_iota(i32, picked, 1) + 1).astype(f32)
    own_rows = pltpu.make_async_copy(send.at[my_at], got.at[my_at], loc_sem.at[3])

    def pick(q):
        d = near_first[q]
        plane = lax.rem(my_plane + d, planes)
        plane_slots = pl.ds(pl.multiple_of(plane * slots_plane, slots_plane), slots_plane)
        hit = jnp.broadcast_to(places[plane_slots, :][:, None, :], picked) == number
        picker = jnp.where(hit, 1.0, 0.0).astype(bf16).reshape(rows_plane, lanes)
        gated = jnp.where(hit, jnp.broadcast_to(weights[plane_slots, :][:, None, :], picked), 0.0)
        gated = gated.astype(bf16).reshape(rows_plane, lanes)
        plane_rows = pl.ds(pl.multiple_of(plane * rows_plane, rows_plane), rows_plane)
        xs = jnp.dot(picker, rx[:, pl.ds(0, dpart)], preferred_element_type=f32)
        cs = jnp.dot(gated, rx[:, pl.ds(dpart, fpart)], preferred_element_type=f32)
        send[plane_rows, pl.ds(0, dpart)] = xs.astype(bf16)
        send[plane_rows, pl.ds(dpart, fpart)] = cs.astype(bf16)

        def dispatch(step, carry):
            slot = plane * slots_plane + lax.rem(here + step, slots_plane)
            pltpu.make_async_remote_copy(
                src_ref=send.at[rows_of(slot)], dst_ref=got.at[my_at],
                send_sem=d_send.at[d], recv_sem=d_recv.at[d],
                device_id={"expert": expert_at(slot)}, device_id_type=MESH,
            ).start()
            return carry

        lax.fori_loop(1 if d == 0 else 0, slots_plane, dispatch, 0)
        if d == 0:
            own_rows.start()

    def ring(kind, q, src, dst, to):
        return pltpu.make_async_remote_copy(
            src_ref=src, dst_ref=dst, send_sem=r_send.at[kind, q], recv_sem=r_recv.at[kind, q],
            device_id={"dp": to}, device_id_type=MESH,
        )

    head, tail = pl.ds(0, half), pl.ds(half, half)
    at_plane = [
        pl.multiple_of(lax.rem(my_plane + planes - d, planes) * rows_plane, rows_plane) for d in near_first
    ]
    pending, settled = [], []

    def go(copy):
        copy.start()
        pending.append(copy)
        return copy

    copies = {}

    def bytes_of(blocks):
        return got.at[pl.ds(0, blocks * per_slot)]

    def partials(q):
        d = near_first[q]
        blocks = slots_plane - 1 if d == 0 else slots_plane
        pltpu.make_async_copy(bytes_of(blocks), bytes_of(blocks), d_recv.at[d]).wait()
        if d == 0:
            own_rows.wait()
        if q == planes - 1:
            rows_out = got.at[pl.ds(at_plane[q], rows_plane), pl.ds(0, dpart)]
            copies["x"] = pltpu.make_async_copy(rows_out, x_last, loc_sem.at[6])
            copies["x"].start()
        x = got[pl.ds(at_plane[q], rows_plane), pl.ds(0, dpart)]

        def part(r):
            cols = pl.ds(pl.multiple_of(r * fpart, 128), fpart)
            return jnp.dot(x, w_own[:, cols], preferred_element_type=f32)

        z_send[0, q] = part(opp).astype(bf16)
        copies[0, q] = go(ring(0, q, z_send.at[0, q, head], z_first.at[0, q], right))
        copies[1, q] = go(ring(1, q, z_send.at[0, q, tail], z_first.at[1, q], left))
        z_send[1, q] = part(right).astype(bf16)
        copies[2, q] = go(ring(2, q, z_send.at[1, q, tail], z_left_in.at[q, tail], right))
        z_send[2, q] = part(left).astype(bf16)
        copies[3, q] = go(ring(3, q, z_send.at[2, q, head], z_right_in.at[q, head], left))
        z_own[q] = part(me_d)

    def pass_on(q):
        copies[0, q].wait_recv()
        z_send[1, q, head] = (z_send[1, q, head].astype(f32) + z_first[0, q].astype(f32)).astype(bf16)
        copies[4, q] = go(ring(4, q, z_send.at[1, q, head], z_left_in.at[q, head], right))
        copies[1, q].wait_recv()
        z_send[2, q, tail] = (z_send[2, q, tail].astype(f32) + z_first[1, q].astype(f32)).astype(bf16)
        copies[5, q] = go(ring(5, q, z_send.at[2, q, tail], z_right_in.at[q, tail], left))

    def finish(q):
        for kind in (2, 3, 4, 5):
            copies[kind, q].wait_recv()
        z = z_own[q] + z_left_in[q].astype(f32) + z_right_in[q].astype(f32)
        sigm = 1.0 / (1.0 + jnp.exp(-z))
        g_cot = got[pl.ds(at_plane[q], rows_plane), pl.ds(dpart, fpart)].astype(f32)
        slope = (g_cot * sigm * (1.0 + z * (1.0 - sigm))).astype(bf16)
        if q < planes - 1:
            slopes[q, me_d] = slope
            src = slopes.at[q, me_d]
        else:
            for kind in (0, 1):
                copies[kind, q].wait_send()
                settled.append(copies[kind, q])
            z_send[0, q] = slope
            src = z_send.at[0, q]
            copies["s"] = pltpu.make_async_copy(src, s_last.at[me_d], loc_sem.at[5])
            copies["s"].start()
        at = block_of(q, me_d, 0, rows_plane)
        copies[6, q] = go(ring(6, q, src, at, right))
        copies[7, q] = go(ring(7, q, src, at, left))

    def block_of(q, dp, first, height):
        held = slopes.at[q] if q < planes - 1 else s_last
        return held.at[dp, pl.ds(first, height)]

    def forward(q):
        copies[6, q].wait_recv()
        at = block_of(q, left, 0, half)
        copies[8, q] = go(ring(8, q, at, at, right))
        copies[7, q].wait_recv()
        at = block_of(q, right, half, half)
        copies[9, q] = go(ring(9, q, at, at, left))

    def gradient(q):
        copies[8, q].wait_recv()
        copies[9, q].wait_recv()
        x = got[pl.ds(at_plane[q], rows_plane), pl.ds(0, dpart)]
        for r in range(nd):
            cols = pl.ds(r * fpart, fpart)
            more = lax.dot_general(x, slopes[q, r], (((0,), (0,)), ((), ())), preferred_element_type=f32)
            if q == 0:
                g_sum[:, cols] = more
            else:
                g_sum[:, cols] = g_sum[:, cols] + more

    for step, q in order:
        (partials, pass_on, finish, forward, moments, gradient, pick)[step](q)

    g_save = pltpu.make_async_copy(g_sum, g_out, loc_sem.at[7])
    g_save.start()

    copies[8, planes - 1].wait_recv()
    copies[9, planes - 1].wait_recv()
    for copy in pending + exchanged:
        if not any(copy is other for other in settled):
            copy.wait_send()
    for d in near_first:
        blocks = slots_plane - 1 if d == 0 else slots_plane
        pltpu.make_async_copy(bytes_of(blocks), bytes_of(blocks), d_send.at[d]).wait()
    copies["x"].wait()
    copies["s"].wait()
    g_save.wait()
    w_save.wait()
    for kind, target in ((1, m_in), (2, v_in)):
        pltpu.make_async_copy(target, target, swap_recv.at[kind]).wait()
        pltpu.make_async_copy(target, target, swap_send.at[kind]).wait()


def exchange(nd, ne, count, ids, gates, flags, tokens, cot, w, m, v):
    tok_rows, width = tokens.shape
    hidden = cot.shape[1]
    dpart, fpart = width // nd, hidden // nd
    planes = 4
    rows = ne * nd * most
    rows_plane = rows // planes
    half = rows_plane // 2
    top = ids.shape[0]
    vm = pl.BlockSpec(memory_space=pltpu.VMEM)
    hbm = pl.BlockSpec(memory_space=pl.ANY)
    state = jax.ShapeDtypeStruct((dpart, hidden), bf16)
    dma = pltpu.SemaphoreType.DMA
    return pl.pallas_call(
        functools.partial(exchange_kernel, nd, ne, planes),
        out_shape=(
            jax.ShapeDtypeStruct((rows_plane, dpart), bf16),
            jax.ShapeDtypeStruct((nd, rows_plane, fpart), bf16),
            jax.ShapeDtypeStruct((dpart, hidden), f32),
            state, state, state,
        ),
        in_specs=[pl.BlockSpec(memory_space=pltpu.SMEM)] + [vm] * 3 + [hbm] * 5,
        out_specs=(hbm,) * 6,
        scratch_shapes=[
            pltpu.VMEM((2 * nd * tok_rows, dpart + fpart), bf16),
            pltpu.VMEM((3 * top, tok_rows), f32),
            pltpu.VMEM((2 * nd, 3 * top, tok_rows), f32),
            pltpu.VMEM((ne // 2, 2 * nd * tok_rows), f32),
            pltpu.VMEM((ne // 2, 2 * nd * tok_rows), f32),
            pltpu.VMEM((rows, dpart + fpart), bf16),
            pltpu.VMEM((rows, dpart + fpart), bf16),
            pltpu.VMEM((dpart, hidden), bf16),
            pltpu.VMEM((dpart, hidden), bf16),
            pltpu.VMEM((3, planes, rows_plane, fpart), bf16),
            pltpu.VMEM((planes, rows_plane, fpart), f32),
            pltpu.VMEM((2, planes, half, fpart), bf16),
            pltpu.VMEM((planes, rows_plane, fpart), bf16),
            pltpu.VMEM((planes, rows_plane, fpart), bf16),
            pltpu.VMEM((planes - 1, nd, rows_plane, fpart), bf16),
            pltpu.VMEM((dpart, hidden), f32),
            dma((10,)), dma((3,)), dma((3,)), dma((3, 4)), dma((3, 4)),
            dma((2 * nd - 1,)), dma((2 * nd - 1,)), dma((3, 3)), dma((3, 3)),
            dma((planes,)), dma((planes,)), dma((10, planes)), dma((10, planes)),
        ],
        compiler_params=pltpu.CompilerParams(collective_id=0, has_side_effects=True, vmem_limit_bytes=56 << 20),
    )(count, ids, gates, flags, tokens, cot, w, m, v)


def update_kernel(flags, me, x, slopes, g, w, m, v, m_in, v_in, w_new, m_new, v_new):
    swapped = flags[me[0]] == 1
    nd, _, fpart = slopes.shape

    def step(first_of, second_of):
        for r in range(nd):
            cols = pl.ds(r * fpart, fpart)
            last = lax.dot_general(x[...], slopes[r], (((0,), (0,)), ((), ())), preferred_element_type=f32)
            grad = g[:, cols] + last
            first_new = beta_first * first_of(cols).astype(f32) + (1.0 - beta_first) * grad
            second_new = beta_second * second_of(cols).astype(f32) + (1.0 - beta_second) * grad * grad
            scaled = second_new * (1.0 / bias_second)
            ratio = first_new * (learn_rate / bias_first) / (scaled * lax.rsqrt(scaled) + epsilon)
            w_new[0, :, cols] = (w[:, cols].astype(f32) - ratio).astype(bf16)
            m_new[0, :, cols] = first_new.astype(bf16)
            v_new[0, :, cols] = second_new.astype(bf16)

    @pl.when(swapped)
    def _():
        step(lambda cols: m_in[:, cols], lambda cols: v_in[:, cols])

    @pl.when(jnp.logical_not(swapped))
    def _():
        step(lambda cols: m[0, :, cols], lambda cols: v[0, :, cols])


def update(flags, me, x, slopes, g, w, m, v, m_in, v_in):
    rows, dpart = x.shape
    nd, _, fpart = slopes.shape
    hidden = nd * fpart
    block = 128
    state = jax.ShapeDtypeStruct((1, dpart, hidden), bf16)
    here = pl.BlockSpec((1, block, hidden), lambda i, flags, me: (0, i, 0))
    stays = pl.BlockSpec((1, block, hidden), lambda i, flags, me: (0, i * (1 - flags[me[0]]), 0))
    moved = pl.BlockSpec((block, hidden), lambda i, flags, me: (i * flags[me[0]], 0))
    return pl.pallas_call(
        update_kernel,
        out_shape=(state, state, state),
        grid_spec=pltpu.PrefetchScalarGridSpec(
            num_scalar_prefetch=2,
            grid=(dpart // block,),
            in_specs=[
                pl.BlockSpec((rows, block), lambda i, flags, me: (0, i)),
                pl.BlockSpec((nd, rows, fpart), lambda i, flags, me: (0, 0, 0)),
                pl.BlockSpec((block, hidden), lambda i, flags, me: (i, 0)),
                pl.BlockSpec((block, hidden), lambda i, flags, me: (i, 0)),
                stays, stays, moved, moved,
            ],
            out_specs=(here, here, here),
        ),
        compiler_params=pltpu.CompilerParams(vmem_limit_bytes=60 << 20),
    )(flags, me, x, slopes, g, w, m, v, m_in, v_in)


def shards(tokens, cotangent, expert_ids, gate_values, counts, swap_flags, weights, first_moment, second_moment):
    ne, nd = lax.axis_size("expert"), lax.axis_size("dp")
    x, slopes, g, w_in, m_in, v_in = exchange(
        nd, ne, counts, expert_ids.T, gate_values.T, swap_flags[None], tokens, cotangent, weights, first_moment, second_moment
    )
    me = lax.axis_index("expert").astype(i32)[None]
    return update(swap_flags, me, x, slopes, g, w_in, first_moment, second_moment, m_in, v_in)


def solution(mesh):
    placed = (
        P(("dp", "expert"), None),
        P(("dp", "expert"), None),
        P(("dp", "expert"), None),
        P(("dp", "expert"), None),
        P(("dp", "expert")),
        P(),
        P("expert", "dp", None),
        P("expert", "dp", None),
        P("expert", "dp", None),
    )
    return jax.shard_map(
        shards,
        mesh=mesh,
        in_specs=placed,
        out_specs=(P("expert", "dp", None), P("expert", "dp", None), P("expert", "dp", None)),
        check_vma=False,
    )
```

```python
import functools

import jax
import jax.numpy as jnp
from jax import lax
from jax.experimental import pallas as pl
from jax.experimental.pallas import tpu as pltpu
from jax.sharding import PartitionSpec as P

beta_first = 0.9
beta_second = 0.95
bias_first = 1.0 - 0.9**3
bias_second = 1.0 - 0.95**3
learn_rate = 0.005
epsilon = 1e-08
most = 6
f32, bf16, i32 = jnp.float32, jnp.bfloat16, jnp.int32
MESH = pl.DeviceIdType.MESH
near_first = (0, 1, 3, 2)
pieces = ((0, 0, 256), (0, 256, 640), (1, 0, 896))
PART, PASS, FINISH, FORWARD, MOMENTS, GRAD, PICK = range(7)
order = (
    (PICK, 0), (PICK, 1), (PICK, 2), (PART, 0), (PICK, 3), (PASS, 0), (FINISH, 0), (PART, 1), (PASS, 1), (FORWARD, 0), (PART, 2), (MOMENTS, 1), (MOMENTS, 2), (FINISH, 1), (PASS, 2), (PART, 3), (PASS, 3), (FORWARD, 1), (FINISH, 2), (GRAD, 0), (FORWARD, 2), (FINISH, 3), (GRAD, 1), (FORWARD, 3), (GRAD, 2),
)


def exchange_kernel(
    nd, ne, planes,
    count, ids, gates, flags, tokens, cot, w, m, v,
    x_last, s_last, g_out, w_in, m_in, v_in,
    rx, aux, aux_in, places, weights, send, got, w_own, w_mov, z_send, z_own, z_first, z_right_in, z_left_in, slopes, g_sum,
    loc_sem, swap_send, swap_recv, ex_send, ex_recv, a_send, a_recv, f_send, f_recv, d_send, d_recv, r_send, r_recv,
):
    me_d, me_e = lax.axis_index("dp"), lax.axis_index("expert")
    right, left, opp = lax.rem(me_d + 1, nd), lax.rem(me_d + nd - 1, nd), lax.rem(me_d + 2, nd)
    mate = lax.rem(me_e + ne // 2, ne)
    top, tok_rows = ids.shape
    dpart, fpart = tokens.shape[1] // nd, cot.shape[1] // nd
    my_z = lax.rem(me_e // 2, 2)
    pair = me_e + 2 - 4 * my_z
    here = (me_e // 4) * 2 + lax.rem(me_e, 2)
    nh = ne // 2
    sources = 2 * nd
    per_slot = sources * most
    slots_plane = nh // planes
    my_plane = here // slots_plane

    def expert_at(spot):
        return (spot // 2) * 4 + 2 * my_z + lax.rem(spot, 2)

    rows_plane = slots_plane * per_slot
    half = rows_plane // 2

    barrier = pltpu.get_barrier_semaphore()

    def greet(i, carry):
        spot = lax.rem(here + i, nh)
        pl.semaphore_signal(barrier, inc=1, device_id={"expert": expert_at(spot)}, device_id_type=MESH)
        return carry

    lax.fori_loop(1, nh, greet, 0)
    others = [(i, e) for i in range(nd) for e in (me_e, pair)][1:]
    for i, e in others:
        pl.semaphore_signal(barrier, inc=1, device_id={"dp": lax.rem(me_d + i, nd), "expert": e}, device_id_type=MESH)
    pl.semaphore_wait(barrier, nh - 1 + len(others))

    def swap(kind, src, dst):
        return pltpu.make_async_remote_copy(
            src_ref=src, dst_ref=dst, send_sem=swap_send.at[kind], recv_sem=swap_recv.at[kind],
            device_id={"expert": mate}, device_id_type=MESH,
        )

    w_swap = swap(0, w.at[0], w_mov)

    def remote(src, dst, send_sem, recv_sem, dp, expert):
        return pltpu.make_async_remote_copy(
            src_ref=src, dst_ref=dst, send_sem=send_sem, recv_sem=recv_sem,
            device_id={"dp": dp, "expert": expert}, device_id_type=MESH,
        )

    def rows_from(dp, z):
        return pl.ds(pl.multiple_of((z * nd + dp) * tok_rows, tok_rows), tok_rows)

    my_rows = rows_from(me_d, my_z)
    side = lax.rem(me_d + nd - 1 + 2 * my_z, nd)

    def tok_cols(r):
        return pl.ds(pl.multiple_of(r * dpart, 128), dpart)

    def cot_cols(r):
        return pl.ds(pl.multiple_of(r * fpart, 128), fpart)

    exchanged = []
    low, high = me_e - 2 * my_z, me_e - 2 * my_z + 2
    split = tok_rows // 2
    parts = ((0, split, 0, dpart), (split, split, 0, dpart), (0, tok_rows, dpart, fpart))

    def part_of(kind, first):
        row, height, col, wide = parts[kind]
        return rx.at[pl.ds(pl.multiple_of(first + row, split), height), pl.ds(col, wide)]

    def first_row(dp, z):
        return (z * nd + dp) * tok_rows

    for kind, (row, height, col, wide) in enumerate(parts):
        for way, (dp, expert, number) in enumerate(
            ((opp, pair, 2), (right, low, my_z), (left, high, my_z), (me_d, pair, 3))
        ):
            src = tokens.at[pl.ds(row, height), tok_cols(dp)] if col == 0 else cot.at[:, cot_cols(dp)]
            dst = part_of(kind, first_row(me_d, my_z))
            copy = remote(src, dst, ex_send.at[kind, way], ex_recv.at[kind, number], dp, expert)
            copy.start()
            exchanged.append(copy)
    def moments(q):
        kind, first, height = pieces[q]
        source, target = ((m, m_in), (v, v_in))[kind]
        at = pl.ds(first, height)
        swap(1 + kind, source.at[0, at], target.at[at]).start()

    w_swap.start()
    moments(0)
    own_x = pltpu.make_async_copy(tokens.at[:, tok_cols(me_d)], rx.at[my_rows, pl.ds(0, dpart)], loc_sem.at[0])
    own_c = pltpu.make_async_copy(cot.at[:, cot_cols(me_d)], rx.at[my_rows, pl.ds(dpart, fpart)], loc_sem.at[1])
    own_w = pltpu.make_async_copy(w.at[0], w_own, loc_sem.at[2])
    own_x.start()
    own_c.start()
    own_w.start()

    experts_col = lax.broadcasted_iota(i32, (ne, tok_rows), 0)
    live = lax.broadcasted_iota(i32, (ne, tok_rows), 1) < count[0]
    every = jnp.zeros((ne, tok_rows), f32)
    for k in range(top):
        every = every + jnp.where((ids[pl.ds(k, 1), :] == experts_col) & live, 1.0, 0.0)
    earlier = jnp.where(
        lax.broadcasted_iota(i32, (tok_rows, tok_rows), 0) < lax.broadcasted_iota(i32, (tok_rows, tok_rows), 1), 1.0, 0.0
    )
    ranked = jnp.dot(every.astype(bf16), earlier.astype(bf16), preferred_element_type=f32)
    flag_row = jnp.broadcast_to(flags[...], (ne, ne))
    expert_row = lax.broadcasted_iota(i32, (ne, ne), 0)
    flag_col = jnp.sum(jnp.where(expert_row == lax.broadcasted_iota(i32, (ne, ne), 1), flag_row, 0), axis=1, keepdims=True)
    expert_col = lax.broadcasted_iota(i32, (ne, 1), 0)
    slot_col = jnp.where(flag_col == 1, lax.rem(expert_col + ne // 2, ne), expert_col).astype(f32) + 1.0
    for k in range(top):
        hit = (ids[pl.ds(k, 1), :] == experts_col) & live
        slot = jnp.sum(jnp.where(hit, slot_col, 0.0), axis=0, keepdims=True)
        rank = jnp.sum(jnp.where(hit, ranked, 0.0), axis=0, keepdims=True)
        aux[pl.ds(k, 1), :] = slot - 1.0
        aux[pl.ds(top + k, 1), :] = rank + ((my_z * nd + me_d) * most + 1)
    aux[pl.ds(2 * top, top), :] = gates[...]
    my_source = my_z * nd + me_d
    aux_in[my_source] = aux[...]
    for n, (i, e) in enumerate(others):
        copy = remote(aux, aux_in.at[my_source], a_send.at[n], a_recv.at[n], lax.rem(me_d + i, nd), e)
        copy.start()
        exchanged.append(copy)

    for kind in range(len(parts)):
        for number, dp, z in ((1 - my_z, side, 1 - my_z), (my_z, side, my_z), (2, opp, 1 - my_z)):
            at = part_of(kind, first_row(dp, z))
            pltpu.make_async_copy(at, at, ex_recv.at[kind, number]).wait()
            copy = remote(at, at, f_send.at[kind, number], f_recv.at[kind, number], me_d, pair)
            copy.start()
            exchanged.append(copy)
    own_w.wait()
    w_swap.wait()
    steps = 7
    w_rows = w_own.shape[0] // steps

    mine = lax.broadcasted_iota(i32, (1, ne), 1) == me_e
    own_flag = jnp.sum(jnp.where(mine, flags[...], 0), axis=1, keepdims=True)

    def choose(i, carry):
        at = pl.ds(pl.multiple_of(i * w_rows, w_rows), w_rows)
        w_own[at] = jnp.where(own_flag == 1, w_mov[at].astype(f32), w_own[at].astype(f32)).astype(bf16)
        return carry

    lax.fori_loop(0, steps, choose, 0)
    w_save = pltpu.make_async_copy(w_own, w_in, loc_sem.at[4])
    w_save.start()

    own_x.wait()
    own_c.wait()
    for kind in range(len(parts)):
        at = part_of(kind, 0)
        pltpu.make_async_copy(at, at, ex_recv.at[kind, 3]).wait()
        for number in range(3):
            pltpu.make_async_copy(at, at, f_recv.at[kind, number]).wait()
    for n in range(len(others)):
        pltpu.make_async_copy(aux, aux, a_recv.at[n]).wait()

    lanes = sources * tok_rows
    to_slot, to_row, gate = (
        jnp.concatenate([aux_in[g, pl.ds(part * top, top), :] for g in range(sources)], axis=1) for part in range(3)
    )
    slots = expert_at(lax.broadcasted_iota(i32, (nh, lanes), 0)).astype(f32)
    place = jnp.zeros((nh, lanes), f32)
    scale = jnp.zeros((nh, lanes), f32)
    for k in range(top):
        hit = slots == to_slot[k : k + 1]
        place = jnp.where(hit, to_row[k : k + 1], place)
        scale = jnp.where(hit, gate[k : k + 1], scale)
    places[...] = place
    weights[...] = scale
    my_at = pl.ds(pl.multiple_of(here * per_slot, per_slot), per_slot)

    def rows_of(slot):
        return pl.ds(pl.multiple_of(slot * per_slot, per_slot), per_slot)

    picked = (slots_plane, per_slot, lanes)
    number = (lax.broadcasted_iota(i32, picked, 1) + 1).astype(f32)
    own_rows = pltpu.make_async_copy(send.at[my_at], got.at[my_at], loc_sem.at[3])

    def pick(q):
        d = near_first[q]
        plane = lax.rem(my_plane + d, planes)
        plane_slots = pl.ds(pl.multiple_of(plane * slots_plane, slots_plane), slots_plane)
        hit = jnp.broadcast_to(places[plane_slots, :][:, None, :], picked) == number
        picker = jnp.where(hit, 1.0, 0.0).astype(bf16).reshape(rows_plane, lanes)
        gated = jnp.where(hit, jnp.broadcast_to(weights[plane_slots, :][:, None, :], picked), 0.0)
        gated = gated.astype(bf16).reshape(rows_plane, lanes)
        plane_rows = pl.ds(pl.multiple_of(plane * rows_plane, rows_plane), rows_plane)
        xs = jnp.dot(picker, rx[:, pl.ds(0, dpart)], preferred_element_type=f32)
        cs = jnp.dot(gated, rx[:, pl.ds(dpart, fpart)], preferred_element_type=f32)
        send[plane_rows, pl.ds(0, dpart)] = xs.astype(bf16)
        send[plane_rows, pl.ds(dpart, fpart)] = cs.astype(bf16)

        def dispatch(step, carry):
            slot = plane * slots_plane + lax.rem(here + step, slots_plane)
            pltpu.make_async_remote_copy(
                src_ref=send.at[rows_of(slot)], dst_ref=got.at[my_at],
                send_sem=d_send.at[d], recv_sem=d_recv.at[d],
                device_id={"expert": expert_at(slot)}, device_id_type=MESH,
            ).start()
            return carry

        lax.fori_loop(1 if d == 0 else 0, slots_plane, dispatch, 0)
        if d == 0:
            own_rows.start()

    def ring(kind, q, src, dst, to):
        return pltpu.make_async_remote_copy(
            src_ref=src, dst_ref=dst, send_sem=r_send.at[kind, q], recv_sem=r_recv.at[kind, q],
            device_id={"dp": to}, device_id_type=MESH,
        )

    head, tail = pl.ds(0, half), pl.ds(half, half)
    at_plane = [
        pl.multiple_of(lax.rem(my_plane + planes - d, planes) * rows_plane, rows_plane) for d in near_first
    ]
    pending, settled = [], []

    def go(copy):
        copy.start()
        pending.append(copy)
        return copy

    copies = {}

    def bytes_of(blocks):
        return got.at[pl.ds(0, blocks * per_slot)]

    def partials(q):
        d = near_first[q]
        blocks = slots_plane - 1 if d == 0 else slots_plane
        pltpu.make_async_copy(bytes_of(blocks), bytes_of(blocks), d_recv.at[d]).wait()
        if d == 0:
            own_rows.wait()
        if q == planes - 1:
            rows_out = got.at[pl.ds(at_plane[q], rows_plane), pl.ds(0, dpart)]
            copies["x"] = pltpu.make_async_copy(rows_out, x_last, loc_sem.at[6])
            copies["x"].start()
        x = got[pl.ds(at_plane[q], rows_plane), pl.ds(0, dpart)]

        def part(r):
            cols = pl.ds(pl.multiple_of(r * fpart, 128), fpart)
            return jnp.dot(x, w_own[:, cols], preferred_element_type=f32)

        z_send[0, q] = part(opp).astype(bf16)
        copies[0, q] = go(ring(0, q, z_send.at[0, q, head], z_first.at[0, q], right))
        copies[1, q] = go(ring(1, q, z_send.at[0, q, tail], z_first.at[1, q], left))
        z_send[1, q] = part(right).astype(bf16)
        copies[2, q] = go(ring(2, q, z_send.at[1, q, tail], z_left_in.at[q, tail], right))
        z_send[2, q] = part(left).astype(bf16)
        copies[3, q] = go(ring(3, q, z_send.at[2, q, head], z_right_in.at[q, head], left))
        z_own[q] = part(me_d)

    def pass_on(q):
        copies[0, q].wait_recv()
        z_send[1, q, head] = (z_send[1, q, head].astype(f32) + z_first[0, q].astype(f32)).astype(bf16)
        copies[4, q] = go(ring(4, q, z_send.at[1, q, head], z_left_in.at[q, head], right))
        copies[1, q].wait_recv()
        z_send[2, q, tail] = (z_send[2, q, tail].astype(f32) + z_first[1, q].astype(f32)).astype(bf16)
        copies[5, q] = go(ring(5, q, z_send.at[2, q, tail], z_right_in.at[q, tail], left))

    def finish(q):
        for kind in (2, 3, 4, 5):
            copies[kind, q].wait_recv()
        z = z_own[q] + z_left_in[q].astype(f32) + z_right_in[q].astype(f32)
        sigm = 1.0 / (1.0 + jnp.exp(-z))
        g_cot = got[pl.ds(at_plane[q], rows_plane), pl.ds(dpart, fpart)].astype(f32)
        slope = (g_cot * sigm * (1.0 + z * (1.0 - sigm))).astype(bf16)
        if q < planes - 1:
            slopes[q, me_d] = slope
            src = slopes.at[q, me_d]
        else:
            for kind in (0, 1):
                copies[kind, q].wait_send()
                settled.append(copies[kind, q])
            z_send[0, q] = slope
            src = z_send.at[0, q]
            copies["s"] = pltpu.make_async_copy(src, s_last.at[me_d], loc_sem.at[5])
            copies["s"].start()
        at = block_of(q, me_d, 0, rows_plane)
        copies[6, q] = go(ring(6, q, src, at, right))
        copies[7, q] = go(ring(7, q, src, at, left))

    def block_of(q, dp, first, height):
        held = slopes.at[q] if q < planes - 1 else s_last
        return held.at[dp, pl.ds(first, height)]

    def forward(q):
        copies[6, q].wait_recv()
        at = block_of(q, left, 0, half)
        copies[8, q] = go(ring(8, q, at, at, right))
        copies[7, q].wait_recv()
        at = block_of(q, right, half, half)
        copies[9, q] = go(ring(9, q, at, at, left))

    def gradient(q):
        copies[8, q].wait_recv()
        copies[9, q].wait_recv()
        x = got[pl.ds(at_plane[q], rows_plane), pl.ds(0, dpart)]
        for r in range(nd):
            cols = pl.ds(r * fpart, fpart)
            more = lax.dot_general(x, slopes[q, r], (((0,), (0,)), ((), ())), preferred_element_type=f32)
            if q == 0:
                g_sum[:, cols] = more
            else:
                g_sum[:, cols] = g_sum[:, cols] + more

    for step, q in order:
        (partials, pass_on, finish, forward, moments, gradient, pick)[step](q)

    g_save = pltpu.make_async_copy(g_sum, g_out, loc_sem.at[7])
    g_save.start()

    copies[8, planes - 1].wait_recv()
    copies[9, planes - 1].wait_recv()
    for copy in pending + exchanged:
        if not any(copy is other for other in settled):
            copy.wait_send()
    for d in near_first:
        blocks = slots_plane - 1 if d == 0 else slots_plane
        pltpu.make_async_copy(bytes_of(blocks), bytes_of(blocks), d_send.at[d]).wait()
    copies["x"].wait()
    copies["s"].wait()
    g_save.wait()
    w_save.wait()
    for kind, target in ((1, m_in), (2, v_in)):
        pltpu.make_async_copy(target, target, swap_recv.at[kind]).wait()
        pltpu.make_async_copy(target, target, swap_send.at[kind]).wait()


def exchange(nd, ne, count, ids, gates, flags, tokens, cot, w, m, v):
    tok_rows, width = tokens.shape
    hidden = cot.shape[1]
    dpart, fpart = width // nd, hidden // nd
    planes = 4
    rows = ne * nd * most
    rows_plane = rows // planes
    half = rows_plane // 2
    top = ids.shape[0]
    vm = pl.BlockSpec(memory_space=pltpu.VMEM)
    hbm = pl.BlockSpec(memory_space=pl.ANY)
    state = jax.ShapeDtypeStruct((dpart, hidden), bf16)
    dma = pltpu.SemaphoreType.DMA
    return pl.pallas_call(
        functools.partial(exchange_kernel, nd, ne, planes),
        out_shape=(
            jax.ShapeDtypeStruct((rows_plane, dpart), bf16),
            jax.ShapeDtypeStruct((nd, rows_plane, fpart), bf16),
            jax.ShapeDtypeStruct((dpart, hidden), f32),
            state, state, state,
        ),
        in_specs=[pl.BlockSpec(memory_space=pltpu.SMEM)] + [vm] * 3 + [hbm] * 5,
        out_specs=(hbm,) * 6,
        scratch_shapes=[
            pltpu.VMEM((2 * nd * tok_rows, dpart + fpart), bf16),
            pltpu.VMEM((3 * top, tok_rows), f32),
            pltpu.VMEM((2 * nd, 3 * top, tok_rows), f32),
            pltpu.VMEM((ne // 2, 2 * nd * tok_rows), f32),
            pltpu.VMEM((ne // 2, 2 * nd * tok_rows), f32),
            pltpu.VMEM((rows, dpart + fpart), bf16),
            pltpu.VMEM((rows, dpart + fpart), bf16),
            pltpu.VMEM((dpart, hidden), bf16),
            pltpu.VMEM((dpart, hidden), bf16),
            pltpu.VMEM((3, planes, rows_plane, fpart), bf16),
            pltpu.VMEM((planes, rows_plane, fpart), f32),
            pltpu.VMEM((2, planes, half, fpart), bf16),
            pltpu.VMEM((planes, rows_plane, fpart), bf16),
            pltpu.VMEM((planes, rows_plane, fpart), bf16),
            pltpu.VMEM((planes - 1, nd, rows_plane, fpart), bf16),
            pltpu.VMEM((dpart, hidden), f32),
            dma((10,)), dma((3,)), dma((3,)), dma((3, 4)), dma((3, 4)),
            dma((2 * nd - 1,)), dma((2 * nd - 1,)), dma((3, 3)), dma((3, 3)),
            dma((planes,)), dma((planes,)), dma((10, planes)), dma((10, planes)),
        ],
        compiler_params=pltpu.CompilerParams(collective_id=0, has_side_effects=True, vmem_limit_bytes=56 << 20),
    )(count, ids, gates, flags, tokens, cot, w, m, v)


def update_kernel(flags, me, x, slopes, g, w, m, v, m_in, v_in, w_new, m_new, v_new):
    swapped = flags[me[0]] == 1
    nd, _, fpart = slopes.shape

    def step(first_of, second_of):
        for r in range(nd):
            cols = pl.ds(r * fpart, fpart)
            last = lax.dot_general(x[...], slopes[r], (((0,), (0,)), ((), ())), preferred_element_type=f32)
            grad = g[:, cols] + last
            first_new = beta_first * first_of(cols).astype(f32) + (1.0 - beta_first) * grad
            second_new = beta_second * second_of(cols).astype(f32) + (1.0 - beta_second) * grad * grad
            scaled = second_new * (1.0 / bias_second)
            ratio = first_new * (learn_rate / bias_first) / (scaled * lax.rsqrt(scaled) + epsilon)
            w_new[0, :, cols] = (w[:, cols].astype(f32) - ratio).astype(bf16)
            m_new[0, :, cols] = first_new.astype(bf16)
            v_new[0, :, cols] = second_new.astype(bf16)

    @pl.when(swapped)
    def _():
        step(lambda cols: m_in[:, cols], lambda cols: v_in[:, cols])

    @pl.when(jnp.logical_not(swapped))
    def _():
        step(lambda cols: m[0, :, cols], lambda cols: v[0, :, cols])


def update(flags, me, x, slopes, g, w, m, v, m_in, v_in):
    rows, dpart = x.shape
    nd, _, fpart = slopes.shape
    hidden = nd * fpart
    block = 128
    state = jax.ShapeDtypeStruct((1, dpart, hidden), bf16)
    here = pl.BlockSpec((1, block, hidden), lambda i, flags, me: (0, i, 0))
    stays = pl.BlockSpec((1, block, hidden), lambda i, flags, me: (0, i * (1 - flags[me[0]]), 0))
    moved = pl.BlockSpec((block, hidden), lambda i, flags, me: (i * flags[me[0]], 0))
    return pl.pallas_call(
        update_kernel,
        out_shape=(state, state, state),
        grid_spec=pltpu.PrefetchScalarGridSpec(
            num_scalar_prefetch=2,
            grid=(dpart // block,),
            in_specs=[
                pl.BlockSpec((rows, block), lambda i, flags, me: (0, i)),
                pl.BlockSpec((nd, rows, fpart), lambda i, flags, me: (0, 0, 0)),
                pl.BlockSpec((block, hidden), lambda i, flags, me: (i, 0)),
                pl.BlockSpec((block, hidden), lambda i, flags, me: (i, 0)),
                stays, stays, moved, moved,
            ],
            out_specs=(here, here, here),
        ),
        compiler_params=pltpu.CompilerParams(vmem_limit_bytes=60 << 20),
    )(flags, me, x, slopes, g, w, m, v, m_in, v_in)


def shards(tokens, cotangent, expert_ids, gate_values, counts, swap_flags, weights, first_moment, second_moment):
    ne, nd = lax.axis_size("expert"), lax.axis_size("dp")
    x, slopes, g, w_in, m_in, v_in = exchange(
        nd, ne, counts, expert_ids.T, gate_values.T, swap_flags[None], tokens, cotangent, weights, first_moment, second_moment
    )
    me = lax.axis_index("expert").astype(i32)[None]
    return update(swap_flags, me, x, slopes, g, w_in, first_moment, second_moment, m_in, v_in)


def solution(mesh):
    placed = (
        P(("dp", "expert"), None),
        P(("dp", "expert"), None),
        P(("dp", "expert"), None),
        P(("dp", "expert"), None),
        P(("dp", "expert")),
        P(),
        P("expert", "dp", None),
        P("expert", "dp", None),
        P("expert", "dp", None),
    )
    return jax.shard_map(
        shards,
        mesh=mesh,
        in_specs=placed,
        out_specs=(P("expert", "dp", None), P("expert", "dp", None), P("expert", "dp", None)),
        check_vma=False,
    )
```
